128 devices in a mesh: tu: 16 (over x, z), tv: 8 (over y, core).
Axes of the slice: x: 4, y: 4, z: 4, core: 2. Of those that a mesh axis runs over, the one named last changes fastest.
Arguments:
- aperture_amp: bfloat16 [512, 512, 512], P(('tu', 'tv')), may hold values from 0.19921875 to 1.796875
- aperture_phase: bfloat16 [512, 512, 512], P(('tu', 'tv')), may hold values from -3.140625 to 3.140625
- plane_depths: float32 [4], replicated, may hold values from 8 to 344
- send_list: int32 [128, 128, 2], P(('tu', 'tv')), may hold values from 0 to 15, as said below
- send_count: int32 [128, 128], P(('tu', 'tv')), may hold values from 0 to 2, as said below
- vis_left: bfloat16 [49152, 128, 128], P(('tu', 'tv')), may hold values from -0.078125 to 0.078125
- vis_right: bfloat16 [49152, 64, 128], P(('tu', 'tv')), may hold values from -0.75 to 0.75
- block_slot: int32 [49152], P(('tu', 'tv')), may hold values from 0 to 255, as said below
- block_pos: int32 [49152], P(('tu', 'tv')), may hold values from 0 to 31
- block_count: int32 [128], P(('tu', 'tv')), may hold values from 96 to 384, as said below
Outputs:
- uv_grid: float32 [2, 4096, 4096], P(None, 'tu', 'tv')
The draws below stay inside these ranges and needn't reach their ends.
Inputs may be any that keep to these rules, and one draw needn't show every extreme that they name: `send_list`: each owner sends every one of its kernels to 8 slots, 128 in all; the used slots of an owner and tile are the first send_count of them; entries of unused slots are arbitrary kernel numbers in range. One tile, drawn afresh, receives 2 slots from every owner; a row of send_count sums to 128. `block_slot`: names a slot r = d * 2 + c that the block's tile receives, with c < send_count[d, tile]. `block_count`: some tile uses all 384 slots.
All inputs are finite; a program needn't handle non-finite values.
Results may differ from the reference program's by a relative error of at most 0.0065.
Values may be sent and summed in bfloat16 or wider, within the bound.
A program may use at most 192 MiB of HBM per device.

```python
import math
import jax
import jax.numpy as jnp
from jax import lax

SCREEN = 512
KSIZE = 64
PATCH = 128
W_PLANES = 4
K_DEV = 16
CAP = 2
FAN = 8
B_DEV = 384
TILE_U = 256
TILE_V = 512
SCREENS = 512
BLOCKS = 49152
NU = 4096
NV = 4096
N_TU = 16
N_TV = 8
DEVICES = 128


def draw_plane_depths(key, part):
    planes = jnp.arange(W_PLANES, dtype=jnp.int32).astype(jnp.float32)
    jitter = jax.random.uniform(jax.random.fold_in(key, 53), (W_PLANES,), jnp.float32)
    units = 12.0 * planes + 1.0 + 6.0 * jitter
    return (units * (SCREEN / 64.0)).astype(jnp.float32)


def routing(key):
    slot_total = DEVICES * CAP
    sends = K_DEV * FAN
    favored = jax.random.randint(jax.random.fold_in(key, 7), (), 0, DEVICES)

    def per_source(source):
        source_key = jax.random.fold_in(jax.random.fold_in(key, 11), source)
        permuted = jax.random.permutation(source_key, slot_total).astype(jnp.int32)
        scores = jnp.where(permuted // CAP == favored, -1, jnp.arange(slot_total, dtype=jnp.int32))
        ordering = jnp.argsort(scores, stable=True)
        dest_seq = permuted[ordering][:sends] // CAP
        onehot = (dest_seq[:, None] == jnp.arange(DEVICES, dtype=jnp.int32)[None, :]).astype(jnp.int32)
        before = jnp.cumsum(onehot, axis=0) - onehot
        slot_ids = jnp.sum(before * onehot, axis=1)
        counts = jnp.sum(onehot, axis=0)
        kernel_ids = jnp.arange(sends, dtype=jnp.int32) // FAN
        filler = jax.random.randint(jax.random.fold_in(source_key, 3), (DEVICES, CAP), 0, K_DEV)
        lists = filler.at[dest_seq, slot_ids].set(kernel_ids)
        return (lists.astype(jnp.int32), counts.astype(jnp.int32))
    return jax.vmap(per_source)(jnp.arange(DEVICES, dtype=jnp.int32))


def draw_send_list(key, part):
    return routing(key)[0]


def draw_send_count(key, part):
    return routing(key)[1]


def draw_block_slot(key, part):
    lists, counts = routing(key)
    is_live = (jnp.arange(CAP, dtype=jnp.int32)[None, None, :] < counts.T[:, :, None]).reshape(DEVICES, DEVICES * CAP).astype(jnp.int32)
    live_total = jnp.sum(is_live, axis=1)
    running = jnp.cumsum(is_live, axis=1)
    random_bits = jax.random.randint(jax.random.fold_in(key, 29), (DEVICES, B_DEV), 0, 2 ** 30)
    chosen = random_bits % jnp.maximum(live_total, 1)[:, None]
    picked = jnp.argmax(running[:, None, :] > chosen[:, :, None], axis=2).astype(jnp.int32)
    return picked.reshape(-1)


def draw_block_count(key, part):
    counts = jax.random.randint(jax.random.fold_in(key, 41), (DEVICES,), B_DEV // 4, B_DEV + 1)
    fullest = jax.random.randint(jax.random.fold_in(key, 43), (), 0, DEVICES)
    return jnp.where(jnp.arange(DEVICES, dtype=jnp.int32) == fullest, B_DEV, counts).astype(jnp.int32)


def touch_ends(drawn, key, smallest, largest):
    dims = drawn.shape
    place = [jax.random.randint(jax.random.fold_in(key, axis), (), 0, dims[axis]) for axis in range(len(dims))]
    drawn = drawn.at[tuple(place)].set(smallest)
    longest = dims.index(max(dims))
    place[longest] = (place[longest] + 1) % dims[longest]
    return drawn.at[tuple(place)].set(largest)


def levels(stream_key, dims, cuts, least, largest):
    factor_of, own = 1.0, jax.random.fold_in(stream_key, 6)
    for axis_at, shards_of in cuts:
        draws = jnp.exp(jax.random.uniform(jax.random.fold_in(own, axis_at), (shards_of,), jnp.float32, least / len(cuts), largest / len(cuts)))
        factor_of = factor_of * jnp.repeat(draws, dims[axis_at] // shards_of).reshape([-1 if axis == axis_at else 1 for axis in range(len(dims))])
    return factor_of


def normal_values(rng, dims, spread, most, pieces=(), kind=jnp.bfloat16):
    values = spread * jax.random.normal(rng, dims, jnp.float32)
    if pieces:
        values = values * levels(rng, dims, pieces, -0.22, 0.18)
    return jnp.clip(values, -most, most).astype(kind)


def setup_inputs(seed: int = 0) -> dict:
    keys = jax.random.split(jax.random.key(seed), 11)
    return {
        "aperture_amp": jnp.clip(0.19921875 + 1.5976562 * jax.random.uniform(keys[0], (SCREENS, SCREEN, SCREEN), jnp.float32) ** levels(keys[0], (SCREENS, SCREEN, SCREEN), ((0, 128),), -0.2, 0.2), 0.19921875, 1.796875).astype(jnp.bfloat16),
        "aperture_phase": jnp.clip(jax.random.uniform(keys[1], (SCREENS, SCREEN, SCREEN), jnp.float32, -3.140625, 3.140625), -3.140625, 3.140625).astype(jnp.bfloat16),
        "plane_depths": draw_plane_depths(jax.random.fold_in(keys[10], 71), 0),
        "send_list": draw_send_list(jax.random.fold_in(keys[10], 71), 0),
        "send_count": draw_send_count(jax.random.fold_in(keys[10], 71), 0),
        "vis_left": normal_values(keys[5], (BLOCKS, PATCH, 2 * KSIZE), (8 * KSIZE * B_DEV * KSIZE * KSIZE // (TILE_U * TILE_V)) ** -0.5, 0.078125, ((0, 128),)),
        "vis_right": normal_values(keys[6], (BLOCKS, KSIZE, PATCH), KSIZE ** -0.5, 0.75, ((0, 128),)),
        "block_slot": draw_block_slot(jax.random.fold_in(keys[10], 71), 0),
        "block_pos": touch_ends(jax.random.randint(keys[8], (BLOCKS,), 0, (TILE_U // KSIZE) * (TILE_V // KSIZE)), jax.random.fold_in(keys[8], 1), 0, ((TILE_U // KSIZE) * (TILE_V // KSIZE)) - 1).astype(jnp.int32),
        "block_count": draw_block_count(jax.random.fold_in(keys[10], 71), 0),
    }


def dft_table(kernel_size, screen_size):
    frequency = jnp.arange(kernel_size, dtype=jnp.int32) - kernel_size // 2
    cell_ids = jnp.arange(screen_size, dtype=jnp.int32)
    turns = jnp.mod(frequency[:, None] * cell_ids[None, :], screen_size).astype(jnp.float32)
    angles = (2.0 * math.pi / screen_size) * turns
    return jnp.concatenate([jnp.cos(angles), -jnp.sin(angles)], axis=0).astype(jnp.bfloat16)


def aperture_screens(amplitude, phase_rows, plane_depths):
    screen_size = amplitude.shape[-1]
    coords = (jnp.arange(screen_size, dtype=jnp.int32).astype(jnp.float32) - screen_size // 2) / screen_size
    radius = coords[:, None] ** 2 + coords[None, :] ** 2
    angles = phase_rows.astype(jnp.float32)[:, None] + (2.0 * math.pi) * plane_depths[None, :, None, None] * radius
    magnitude = amplitude.astype(jnp.float32)[:, None]
    real_part = (magnitude * jnp.cos(angles)).astype(jnp.bfloat16)
    imag_part = (magnitude * jnp.sin(angles)).astype(jnp.bfloat16)
    stacked = jnp.concatenate([real_part, imag_part], axis=-1)
    return stacked.reshape(-1, screen_size, 2 * screen_size)


def kernels_from(stacked, kernel_size):
    screen_size = stacked.shape[1]
    dft = dft_table(kernel_size, screen_size).astype(jnp.float32)
    product = jnp.einsum("as,ksn->kan", dft, stacked.astype(jnp.float32), precision=lax.Precision.HIGHEST)
    half_real = product[:, :kernel_size, :screen_size] - product[:, kernel_size:, screen_size:]
    half_imag = product[:, :kernel_size, screen_size:] + product[:, kernel_size:, :screen_size]
    halves = jnp.concatenate([half_real, half_imag], axis=1).astype(jnp.bfloat16)
    second = jnp.einsum("kas,bs->kab", halves.astype(jnp.float32), dft, precision=lax.Precision.HIGHEST)
    out_real = second[:, :kernel_size, :kernel_size] - second[:, kernel_size:, kernel_size:]
    out_imag = second[:, :kernel_size, kernel_size:] + second[:, kernel_size:, :kernel_size]
    return (jnp.concatenate([out_real, out_imag], axis=-1) / screen_size).astype(jnp.bfloat16)


def grid_patches(block_kernels, left_rows, right_rows):
    kernel_size = block_kernels.shape[1]
    real_k = block_kernels[:, :, :kernel_size]
    imag_k = block_kernels[:, :, kernel_size:]
    operator_rows = jnp.concatenate([block_kernels, jnp.concatenate([-imag_k, real_k], axis=2)], axis=1)
    mixed = jnp.einsum("gpc,gcd->gpd", left_rows.astype(jnp.float32), operator_rows.astype(jnp.float32), precision=lax.Precision.HIGHEST).astype(jnp.bfloat16)
    mixed = mixed.reshape(mixed.shape[0], mixed.shape[1], 2, kernel_size)
    return jnp.einsum("gpck,gkq->gcpq", mixed.astype(jnp.float32), right_rows.astype(jnp.float32), precision=lax.Precision.HIGHEST)


def spread_patches(placed, row_slots, col_slots, kernel_size):
    placed = placed.reshape(row_slots, col_slots, 2, 2, kernel_size, 2, kernel_size)
    extended = jnp.zeros((row_slots + 1, col_slots + 1, 2, kernel_size, kernel_size), jnp.float32)
    for row_shift in range(2):
        for col_shift in range(2):
            extended = extended.at[row_shift:row_shift + row_slots, col_shift:col_shift + col_slots].add(placed[:, :, :, row_shift, :, col_shift, :])
    extended = extended.transpose(2, 0, 3, 1, 4)
    return extended.reshape(2, (row_slots + 1) * kernel_size, (col_slots + 1) * kernel_size)


def reference(aperture_amp, aperture_phase, plane_depths, send_list, send_count, vis_left, vis_right, block_slot, block_pos, block_count):
    devices_total = N_TU * N_TV
    row_slots = TILE_U // KSIZE
    col_slots = TILE_V // KSIZE

    def per_screen(screen_pair):
        return kernels_from(aperture_screens(screen_pair[0][None], screen_pair[1][None], plane_depths), KSIZE)

    kernels = lax.map(per_screen, (aperture_amp, aperture_phase)).reshape(-1, KSIZE, 2 * KSIZE)
    sources = jnp.arange(devices_total, dtype=jnp.int32)

    def per_tile(tile_in):
        tile_id, left_rows, right_rows, slot_ids, positions, tile_count = tile_in
        chosen = sources[:, None] * K_DEV + send_list[:, tile_id, :]
        is_live = jnp.arange(CAP, dtype=jnp.int32)[None, :] < send_count[:, tile_id][:, None]
        received = jnp.where(is_live[:, :, None, None], kernels[chosen], jnp.zeros((), jnp.bfloat16))
        received = received.reshape(devices_total * CAP, KSIZE, 2 * KSIZE)
        patches = grid_patches(received[slot_ids], left_rows, right_rows)
        block_live = (jnp.arange(B_DEV, dtype=jnp.int32) < tile_count).astype(jnp.float32)
        patches = patches * block_live[:, None, None, None]
        placed = jax.ops.segment_sum(patches, positions, num_segments=row_slots * col_slots)
        return spread_patches(placed, row_slots, col_slots, KSIZE)

    tiles_in = (sources,
                vis_left.reshape(devices_total, B_DEV, PATCH, 2 * KSIZE),
                vis_right.reshape(devices_total, B_DEV, KSIZE, PATCH),
                block_slot.reshape(devices_total, B_DEV),
                block_pos.reshape(devices_total, B_DEV),
                block_count)
    extended = lax.map(per_tile, tiles_in).reshape(N_TU, N_TV, 2, TILE_U + KSIZE, TILE_V + KSIZE)
    bottom = extended[:, :, :, TILE_U:, :]
    moved = jnp.concatenate([jnp.zeros_like(bottom[:1]), bottom[:-1]], axis=0)
    extended = extended.at[:, :, :, :KSIZE, :].add(moved)
    side = extended[:, :, :, :TILE_U, TILE_V:]
    moved = jnp.concatenate([jnp.zeros_like(side[:, :1]), side[:, :-1]], axis=1)
    tiles = extended[:, :, :, :TILE_U, :TILE_V].at[:, :, :, :, :KSIZE].add(moved)
    return tiles.transpose(2, 0, 3, 1, 4).reshape(2, NU, NV)
```

```python
import functools
import math

import jax
import jax.numpy as jnp
import numpy as np
from jax import lax
from jax.experimental import pallas as pl
from jax.experimental.pallas import tpu as pltpu
from jax.sharding import PartitionSpec as P

SCREEN = 512
KSIZE = 64
PATCH = 128
PLANES = 4
SCREENS_DEV = 4
BLOCKS_DEV = 384
OWNERS = 128
TILE_U = 256
TILE_V = 512
POSITIONS = 32
GROUP = 4
MAX_GROUPS = BLOCKS_DEV // GROUP + POSITIONS
DEPTH = 8
EXT_U = TILE_U + KSIZE

SIN = (0.9999995827674866, -0.16666553914546967, 0.008332408033311367,
       -0.00019808740762528032, 2.6998227440344635e-06, -2.036623314438657e-08)
COS = (0.9999992251396179, -0.49999427795410156, 0.041659820824861526,
       -0.0013858915772289038, 2.4204400688176975e-05, -2.19788830690959e-07)


def sincos(x):
    z = x * x
    s = jnp.float32(SIN[-1])
    for c in SIN[-2::-1]:
        s = s * z + c
    k = jnp.float32(COS[-1])
    for c in COS[-2::-1]:
        k = k * z + c
    return s * x, k


def dft_rows():
    freq = np.arange(KSIZE) - KSIZE // 2
    turns = np.mod(freq[:, None] * np.arange(SCREEN)[None, :], SCREEN)
    angles = 2.0 * math.pi / SCREEN * turns
    return np.stack([np.cos(angles), -np.sin(angles)]).astype(np.float32)


def screen_kernel(w_ref, list_ref, amp_ref, phase_ref, f_ref, even_ref, odd_ref,
                  weight, parts, halves, kernels):
    coords = (lax.broadcasted_iota(jnp.int32, (1, SCREEN), 1) - SCREEN // 2).astype(jnp.float32)
    square = coords * coords * (1.0 / (SCREEN * SCREEN))
    for p in range(PLANES):
        turns = square * w_ref[p]
        turns = turns - jnp.floor(turns + 0.5)
        sin_p, cos_p = sincos(turns * (2.0 * math.pi))
        f_re, f_im = f_ref[0], f_ref[1]
        w_re = (f_re * cos_p - f_im * sin_p).astype(jnp.bfloat16)
        w_im = (f_re * sin_p + f_im * cos_p).astype(jnp.bfloat16)
        top = slice(p * 2 * KSIZE, p * 2 * KSIZE + KSIZE)
        low = slice(p * 2 * KSIZE + KSIZE, (p + 1) * 2 * KSIZE)
        weight[top, :SCREEN] = w_re
        weight[top, SCREEN:] = -w_im
        weight[low, :SCREEN] = w_im
        weight[low, SCREEN:] = w_re
    rows = 32
    for s in range(SCREENS_DEV):
        def fill(i, carry):
            at = pl.ds(pl.multiple_of(i * rows, rows), rows)
            sin_v, cos_v = sincos(phase_ref[s, at, :].astype(jnp.float32))
            amp = amp_ref[s, at, :].astype(jnp.float32)
            parts[s % 2, at, :] = (amp * cos_v).astype(jnp.bfloat16)
            parts[s % 2, pl.ds(pl.multiple_of(SCREEN + i * rows, rows), rows), :] = (
                amp * sin_v).astype(jnp.bfloat16)
            return carry
        lax.fori_loop(0, SCREEN // rows, fill, 0)
        for p in range(PLANES):
            half = jnp.dot(weight[p * 128:(p + 1) * 128, :], parts[s % 2],
                           preferred_element_type=jnp.float32).astype(jnp.bfloat16)
            halves[p, s * KSIZE:(s + 1) * KSIZE, :SCREEN] = half[:KSIZE]
            halves[p, s * KSIZE:(s + 1) * KSIZE, SCREEN:] = half[KSIZE:]
    for p in range(PLANES):
        out = lax.dot_general(halves[p], weight[p * 128:(p + 1) * 128, :],
                              (((1,), (1,)), ((), ())), preferred_element_type=jnp.float32)
        out = (out * (1.0 / SCREEN)).astype(jnp.bfloat16)
        for s in range(SCREENS_DEV):
            kernels[s * PLANES + p] = out[s * KSIZE:(s + 1) * KSIZE]

    def deliver(t, carry):
        even_ref[t] = kernels[list_ref[2 * t]]
        odd_ref[t] = kernels[list_ref[2 * t + 1]]
        return carry
    lax.fori_loop(0, OWNERS, deliver, 0)


def make_outgoing(depths, send_list, amp, phase):
    vmem = pl.BlockSpec(memory_space=pltpu.VMEM)
    smem = pl.BlockSpec(memory_space=pltpu.SMEM)
    slots = jax.ShapeDtypeStruct((OWNERS, KSIZE, 2 * KSIZE), jnp.bfloat16)
    return pl.pallas_call(
        screen_kernel,
        out_shape=(slots, slots),
        in_specs=[smem, smem, vmem, vmem, vmem],
        out_specs=(vmem, vmem),
        scratch_shapes=[
            pltpu.VMEM((PLANES * 128, 2 * SCREEN), jnp.bfloat16),
            pltpu.VMEM((2, 2 * SCREEN, SCREEN), jnp.bfloat16),
            pltpu.VMEM((PLANES, SCREENS_DEV * KSIZE, 2 * SCREEN), jnp.bfloat16),
            pltpu.VMEM((SCREENS_DEV * PLANES, KSIZE, 2 * KSIZE), jnp.bfloat16),
        ],
        compiler_params=pltpu.CompilerParams(vmem_limit_bytes=40 << 20),
        cost_estimate=pl.CostEstimate(flops=2_700_000_000, bytes_accessed=8_600_000,
                                      transcendentals=2_000_000),
        name="screens",
    )(depths, send_list.reshape(-1), amp, phase, jnp.asarray(dft_rows()))


def schedule_blocks(block_slot, block_pos, block_count):
    ids = jnp.arange(BLOCKS_DEV, dtype=jnp.int32)
    bins = (block_slot & 1) * POSITIONS + block_pos
    bins = jnp.where(ids < block_count[0], bins, -1)
    hot = (bins[:, None] == jnp.arange(2 * POSITIONS, dtype=jnp.int32)[None, :]).astype(jnp.float32)
    upto = (ids[:, None] >= ids[None, :]).astype(jnp.float32)
    rank = jnp.sum(jnp.dot(upto, hot, preferred_element_type=jnp.float32) * hot, axis=1) - 1.0
    groups = jnp.floor((jnp.sum(hot, axis=0) + (GROUP - 1.0)) * (1.0 / GROUP))
    b = jnp.arange(2 * POSITIONS, dtype=jnp.int32)
    before = (b[:, None] < b[None, :]) & (b[:, None] // POSITIONS == b[None, :] // POSITIONS)
    first = jnp.sum(jnp.where(before, groups[:, None], 0.0), axis=0)
    place = jnp.sum(hot * first[None, :], axis=1) * GROUP + rank
    place = place.astype(jnp.int32) + (block_slot & 1) * (MAX_GROUPS * GROUP)
    place = jnp.where(bins >= 0, place, -1)
    spots = jnp.arange(2 * MAX_GROUPS * GROUP, dtype=jnp.int32)
    code = ids * OWNERS + (block_slot >> 1) + 1
    codes = jnp.sum(jnp.where(place[None, :] == spots[:, None], code[None, :], 0), axis=1)
    last = (first + groups).astype(jnp.int32).reshape(2, 1, POSITIONS)
    anchors = jnp.sum((last <= jnp.arange(MAX_GROUPS, dtype=jnp.int32)[None, :, None]).astype(jnp.int32), axis=2)
    totals = jnp.sum(groups.reshape(2, POSITIONS), axis=1).astype(jnp.int32)
    return codes.reshape(2, -1), anchors, totals


def lanes_low(shape):
    return lax.broadcasted_iota(jnp.int32, shape, len(shape) - 1) < KSIZE


def operator_pair(first, second):
    zero = jnp.zeros((KSIZE, 2 * KSIZE), jnp.bfloat16)
    low = lanes_low((KSIZE, 2 * KSIZE))
    turned = [jnp.concatenate([v[:, KSIZE:], v[:, :KSIZE]], axis=1) for v in (first, second)]
    left = jnp.concatenate([
        jnp.where(low, first, zero), jnp.where(low, -turned[0], zero),
        jnp.where(low, zero, turned[1]), jnp.where(low, zero, -second)], axis=0)
    right = jnp.concatenate([
        jnp.where(low, turned[0], zero), jnp.where(low, first, zero),
        jnp.where(low, zero, second), jnp.where(low, zero, turned[1])], axis=0)
    return jnp.concatenate([left, right], axis=1)


def grid_groups(code_ref, anchor_ref, total_ref, recv, left_hbm, right_hbm, grid, lbuf, rbuf, sems):
    total = total_ref[0]

    def block_of(g, i):
        return jnp.maximum(code_ref[g * GROUP + i] - 1, 0)

    def copies(g, slot):
        out = []
        for i in range(GROUP):
            block = block_of(g, i) >> 7
            out.append(pltpu.make_async_copy(left_hbm.at[block], lbuf.at[slot, i], sems.at[slot, i]))
            out.append(pltpu.make_async_copy(
                right_hbm.at[block], rbuf.at[slot, pl.ds(i * KSIZE, KSIZE)], sems.at[slot, GROUP + i]))
        return out

    def start(g):
        for copy in copies(g, lax.rem(g, DEPTH)):
            copy.start()

    for g in range(DEPTH - 1):
        @pl.when(g < total)
        def _():
            start(g)

    def step(g, carry):
        slot = lax.rem(g, DEPTH)

        @pl.when(g + DEPTH - 1 < total)
        def _():
            start(g + DEPTH - 1)
        for copy in copies(g, slot):
            copy.wait()
        halves = []
        for pair in range(GROUP // 2):
            picked = []
            for i in (2 * pair, 2 * pair + 1):
                k = recv[block_of(g, i) & (OWNERS - 1)]
                used = code_ref[g * GROUP + i] > 0
                picked.append(jnp.where(used, k, jnp.zeros_like(k)))
            rows = jnp.concatenate([lbuf[slot, 2 * pair], lbuf[slot, 2 * pair + 1]], axis=1)
            mixed = jnp.dot(rows, operator_pair(*picked), preferred_element_type=jnp.float32)
            halves.append(mixed.astype(jnp.bfloat16))
        stacked = jnp.concatenate([
            jnp.concatenate([h[:, :PATCH] for h in halves], axis=1),
            jnp.concatenate([h[:, PATCH:] for h in halves], axis=1)], axis=0)
        patch = jnp.dot(stacked, rbuf[slot], preferred_element_type=jnp.float32)
        anchor = anchor_ref[g]
        row = pl.ds(pl.multiple_of((anchor >> 3) * KSIZE, KSIZE), PATCH)
        odd, col = anchor & 1, (anchor & 7) >> 1
        grid[odd, col, 0, row, :] += patch[:PATCH]
        grid[odd, col, 1, row, :] += patch[PATCH:]
        return carry
    lax.fori_loop(0, total, step, 0)


def first_kernel(code, anchor, total, recv, left, right, grid, lbuf, rbuf, sems):
    grid[...] = jnp.zeros_like(grid)
    grid_groups(code, anchor, total, recv, left, right, grid, lbuf, rbuf, sems)


def turn(v):
    return pltpu.roll(v, KSIZE, 1)


def second_kernel(code, anchor, total, recv, left, right, grid_in, main, bottom, side,
                  grid, lbuf, rbuf, sems):
    grid[...] = grid_in[...]
    grid_groups(code, anchor, total, recv, left, right, grid, lbuf, rbuf, sems)
    low = lanes_low((KSIZE, PATCH))
    for plane in range(2):
        for r in range(EXT_U // KSIZE):
            rows = slice(r * KSIZE, (r + 1) * KSIZE)
            shifted = [turn(grid[1, col, plane, rows, :]) for col in range(4)]
            for col in range(4):
                before = shifted[col - 1] if col else jnp.zeros_like(shifted[0])
                value = grid[0, col, plane, rows, :] + jnp.where(low, before, shifted[col])
                cols = slice(col * PATCH, (col + 1) * PATCH)
                if r < TILE_U // KSIZE:
                    main[plane, rows, cols] = value
                else:
                    bottom[plane, :, cols] = value.astype(jnp.bfloat16)
    for r in range(EXT_U // KSIZE):
        rows = slice(r * KSIZE, (r + 1) * KSIZE)
        value = jnp.where(low, turn(grid[1, 3, 0, rows, :]), grid[1, 3, 1, rows, :])
        side[rows, :] = value.astype(jnp.bfloat16)


GRID_SHAPE = (2, 4, 2, EXT_U, PATCH)


def grid_call(kernel, name, out_shape, code, anchor, total, recv, left, right, *more, scratch=()):
    vmem = pl.BlockSpec(memory_space=pltpu.VMEM)
    smem = pl.BlockSpec(memory_space=pltpu.SMEM)
    hbm = pl.BlockSpec(memory_space=pl.ANY)
    return pl.pallas_call(
        kernel,
        out_shape=out_shape,
        in_specs=[smem, smem, smem, vmem, hbm, hbm] + [vmem] * len(more),
        out_specs=jax.tree.map(lambda _: vmem, out_shape),
        scratch_shapes=[*scratch,
                        pltpu.VMEM((DEPTH, GROUP, PATCH, 2 * KSIZE), jnp.bfloat16),
                        pltpu.VMEM((DEPTH, GROUP * KSIZE, PATCH), jnp.bfloat16),
                        pltpu.SemaphoreType.DMA((DEPTH, 2 * GROUP))],
        compiler_params=pltpu.CompilerParams(vmem_limit_bytes=40 << 20),
        cost_estimate=pl.CostEstimate(flops=3_000_000_000, bytes_accessed=12_000_000,
                                      transcendentals=0),
        name=name,
    )(code, anchor, total, recv, left, right, *more)


def join_kernel(main, bottom, side, corner, out):
    low = lanes_low((TILE_U, PATCH))
    out[...] = main[...]
    out[:, :KSIZE, :] += bottom[...].astype(jnp.float32)
    edge = side[...].astype(jnp.float32)
    zero = jnp.zeros_like(edge)
    low_corner = lanes_low((KSIZE, PATCH))
    tip = corner[...].astype(jnp.float32)
    out[0, :, :PATCH] += jnp.where(low, edge, zero)
    out[1, :, :PATCH] += jnp.where(low, turn(edge), zero)
    out[0, :KSIZE, :PATCH] += jnp.where(low_corner, tip, zero[:KSIZE])
    out[1, :KSIZE, :PATCH] += jnp.where(low_corner, turn(tip), zero[:KSIZE])


def shards(aperture_amp, aperture_phase, plane_depths, send_list, send_count, vis_left, vis_right,
           block_slot, block_pos, block_count):
    axes = ("tu", "tv")
    n_tu, n_tv = lax.axis_size("tu"), lax.axis_size("tv")
    even, odd = make_outgoing(plane_depths, send_list, aperture_amp, aperture_phase)
    even = lax.all_to_all(even, axes, split_axis=0, concat_axis=0, tiled=True)
    odd = lax.all_to_all(odd, axes, split_axis=0, concat_axis=0, tiled=True)
    codes, anchors, totals = schedule_blocks(block_slot, block_pos, block_count)
    grid = grid_call(first_kernel, "grid_even", jax.ShapeDtypeStruct(GRID_SHAPE, jnp.float32),
                     codes[0], anchors[0], totals[:1], even, vis_left, vis_right)
    main, bottom, side = grid_call(
        second_kernel, "grid_odd",
        (jax.ShapeDtypeStruct((2, TILE_U, TILE_V), jnp.float32),
         jax.ShapeDtypeStruct((2, KSIZE, TILE_V), jnp.bfloat16),
         jax.ShapeDtypeStruct((EXT_U, PATCH), jnp.bfloat16)),
        codes[1], anchors[1], totals[1:], odd, vis_left, vis_right, grid,
        scratch=(pltpu.VMEM(GRID_SHAPE, jnp.float32),))
    bottom = lax.ppermute(bottom, "tu", [(i, i + 1) for i in range(n_tu - 1)])
    corner = lax.ppermute(side[TILE_U:], axes, [
        (u * n_tv + v, (u + 1) * n_tv + v + 1) for u in range(n_tu - 1) for v in range(n_tv - 1)])
    side = lax.ppermute(side[:TILE_U], "tv", [(i, i + 1) for i in range(n_tv - 1)])
    vmem = pl.BlockSpec(memory_space=pltpu.VMEM)
    return pl.pallas_call(
        join_kernel,
        out_shape=jax.ShapeDtypeStruct((2, TILE_U, TILE_V), jnp.float32),
        in_specs=[vmem] * 4,
        out_specs=vmem,
        compiler_params=pltpu.CompilerParams(vmem_limit_bytes=16 << 20),
        cost_estimate=pl.CostEstimate(flops=1_000_000, bytes_accessed=2_300_000, transcendentals=0),
        name="join_borders",
    )(main, bottom, side, corner)


def solution(mesh):
    placed = (
        P(("tu", "tv"), None, None),
        P(("tu", "tv"), None, None),
        P(),
        P(("tu", "tv"), None, None),
        P(("tu", "tv"), None),
        P(("tu", "tv"), None, None),
        P(("tu", "tv"), None, None),
        P(("tu", "tv")),
        P(("tu", "tv")),
        P(("tu", "tv")),
    )
    return jax.shard_map(
        shards, mesh=mesh, in_specs=placed, out_specs=P(None, "tu", "tv"), check_vma=False
    )
```

```python
import math
import random

import jax
import jax.numpy as jnp
import numpy as np
from jax import lax
from jax.experimental import pallas as pl
from jax.experimental.pallas import tpu as pltpu
from jax.sharding import PartitionSpec as P

SCREEN = 512
KSIZE = 64
PATCH = 128
PLANES = 4
SCREENS_DEV = 4
BLOCKS_DEV = 384
OWNERS = 128
TILE_U = 256
TILE_V = 512
POSITIONS = 32
GROUP = 4
MAX_GROUPS = BLOCKS_DEV // GROUP + POSITIONS
DEPTH = 8
EXT_U = TILE_U + KSIZE

SIN = (0.9999995827674866, -0.16666553914546967, 0.008332408033311367,
       -0.00019808740762528032, 2.6998227440344635e-06, -2.036623314438657e-08)
COS = (0.9999992251396179, -0.49999427795410156, 0.041659820824861526,
       -0.0013858915772289038, 2.4204400688176975e-05, -2.19788830690959e-07)


def sincos(x):
    z = x * x
    s = jnp.float32(SIN[-1])
    for c in SIN[-2::-1]:
        s = s * z + c
    k = jnp.float32(COS[-1])
    for c in COS[-2::-1]:
        k = k * z + c
    return s * x, k


def dft_rows():
    freq = np.arange(KSIZE) - KSIZE // 2
    turns = np.mod(freq[:, None] * np.arange(SCREEN)[None, :], SCREEN)
    angles = 2.0 * math.pi / SCREEN * turns
    return np.stack([np.cos(angles), -np.sin(angles)]).astype(np.float32)


def screen_kernel(w_hbm, list_ref, amp_hbm, phase_hbm, f_hbm, even_hbm, odd_hbm,
                  even_ref, odd_ref,
                  w_ref, f_ref, amp_ref, phase_ref, weight, parts, halves, kernels, sems):
    small = [pltpu.make_async_copy(w_hbm, w_ref, sems.at[0]),
             pltpu.make_async_copy(f_hbm, f_ref, sems.at[1])]
    loads = [(pltpu.make_async_copy(phase_hbm.at[s], phase_ref.at[s], sems.at[2 + 2 * s]),
              pltpu.make_async_copy(amp_hbm.at[s], amp_ref.at[s], sems.at[3 + 2 * s]))
             for s in range(SCREENS_DEV)]
    for copy in small + [c for pair in loads for c in pair]:
        copy.start()
    for copy in small:
        copy.wait()
    coords = (lax.broadcasted_iota(jnp.int32, (1, SCREEN), 1) - SCREEN // 2).astype(jnp.float32)
    square = coords * coords * (1.0 / (SCREEN * SCREEN))
    for p in range(PLANES):
        turns = square * w_ref[p]
        turns = turns - jnp.floor(turns + 0.5)
        sin_p, cos_p = sincos(turns * (2.0 * math.pi))
        f_re, f_im = f_ref[0], f_ref[1]
        w_re = (f_re * cos_p - f_im * sin_p).astype(jnp.bfloat16)
        w_im = (f_re * sin_p + f_im * cos_p).astype(jnp.bfloat16)
        top = slice(p * 2 * KSIZE, p * 2 * KSIZE + KSIZE)
        low = slice(p * 2 * KSIZE + KSIZE, (p + 1) * 2 * KSIZE)
        weight[top, :SCREEN] = w_re
        weight[top, SCREEN:] = -w_im
        weight[low, :SCREEN] = w_im
        weight[low, SCREEN:] = w_re
    rows = 32
    for s in range(SCREENS_DEV):
        for copy in loads[s]:
            copy.wait()

        def fill(i, carry):
            at = pl.ds(pl.multiple_of(i * rows, rows), rows)
            sin_v, cos_v = sincos(phase_ref[s, at, :].astype(jnp.float32))
            amp = amp_ref[s, at, :].astype(jnp.float32)
            parts[s % 2, at, :] = (amp * cos_v).astype(jnp.bfloat16)
            parts[s % 2, pl.ds(pl.multiple_of(SCREEN + i * rows, rows), rows), :] = (
                amp * sin_v).astype(jnp.bfloat16)
            return carry
        lax.fori_loop(0, SCREEN // rows, fill, 0)
        for p in range(PLANES):
            half = jnp.dot(weight[p * 128:(p + 1) * 128, :], parts[s % 2],
                           preferred_element_type=jnp.float32).astype(jnp.bfloat16)
            halves[p, s * KSIZE:(s + 1) * KSIZE, :SCREEN] = half[:KSIZE]
            halves[p, s * KSIZE:(s + 1) * KSIZE, SCREEN:] = half[KSIZE:]
    for p in range(PLANES):
        out = lax.dot_general(halves[p], weight[p * 128:(p + 1) * 128, :],
                              (((1,), (1,)), ((), ())), preferred_element_type=jnp.float32)
        out = (out * (1.0 / SCREEN)).astype(jnp.bfloat16)
        for s in range(SCREENS_DEV):
            kernels[s * PLANES + p] = out[s * KSIZE:(s + 1) * KSIZE]

    outs = []
    for c, (slots, out) in enumerate([(even_ref, even_hbm), (odd_ref, odd_hbm)]):
        def deliver(t, carry):
            slots[t] = kernels[list_ref[c, t]]
            return carry
        lax.fori_loop(0, OWNERS, deliver, 0)
        outs.append(pltpu.make_async_copy(slots, out, sems.at[10 + c]))
        outs[-1].start()
    for copy in outs:
        copy.wait()


def make_outgoing(depths, send_list, amp, phase):
    smem = pl.BlockSpec(memory_space=pltpu.SMEM)
    hbm = pl.BlockSpec(memory_space=pltpu.MemorySpace.HBM)
    slots = jax.ShapeDtypeStruct((OWNERS, KSIZE, 2 * KSIZE), jnp.bfloat16)
    return pl.pallas_call(
        screen_kernel,
        out_shape=(slots, slots),
        in_specs=[hbm, smem] + [hbm] * 3,
        out_specs=(hbm, hbm),
        scratch_shapes=[
            pltpu.VMEM(slots.shape, slots.dtype),
            pltpu.VMEM(slots.shape, slots.dtype),
            pltpu.SMEM((PLANES,), jnp.float32),
            pltpu.VMEM((2, KSIZE, SCREEN), jnp.float32),
            pltpu.VMEM((SCREENS_DEV, SCREEN, SCREEN), jnp.bfloat16),
            pltpu.VMEM((SCREENS_DEV, SCREEN, SCREEN), jnp.bfloat16),
            pltpu.VMEM((PLANES * 128, 2 * SCREEN), jnp.bfloat16),
            pltpu.VMEM((2, 2 * SCREEN, SCREEN), jnp.bfloat16),
            pltpu.VMEM((PLANES, SCREENS_DEV * KSIZE, 2 * SCREEN), jnp.bfloat16),
            pltpu.VMEM((SCREENS_DEV * PLANES, KSIZE, 2 * KSIZE), jnp.bfloat16),
            pltpu.SemaphoreType.DMA((12,)),
        ],
        cost_estimate=pl.CostEstimate(flops=2_700_000_000, bytes_accessed=8_600_000,
                                      transcendentals=2_000_000),
        name="screens",
    )(depths, send_list[0].T, amp, phase, jnp.asarray(dft_rows()))


def schedule_blocks(block_slot, block_pos, block_count):
    ids = jnp.arange(BLOCKS_DEV, dtype=jnp.int32)
    bins = (block_slot & 1) * POSITIONS + block_pos
    bins = jnp.where(ids < block_count[0], bins, -1)
    hot = (bins[:, None] == jnp.arange(2 * POSITIONS, dtype=jnp.int32)[None, :]).astype(jnp.float32)
    upto = (ids[:, None] >= ids[None, :]).astype(jnp.float32)
    rank = jnp.sum(jnp.dot(upto, hot, preferred_element_type=jnp.float32) * hot, axis=1) - 1.0
    groups = jnp.floor((jnp.sum(hot, axis=0) + (GROUP - 1.0)) * (1.0 / GROUP))
    b = jnp.arange(2 * POSITIONS, dtype=jnp.int32)
    before = (b[:, None] < b[None, :]) & (b[:, None] // POSITIONS == b[None, :] // POSITIONS)
    first = jnp.sum(jnp.where(before, groups[:, None], 0.0), axis=0)
    place = jnp.sum(hot * first[None, :], axis=1) * GROUP + rank
    place = place.astype(jnp.int32) + (block_slot & 1) * (MAX_GROUPS * GROUP)
    place = jnp.where(bins >= 0, place, -1)
    spots = jnp.arange(2 * MAX_GROUPS * GROUP, dtype=jnp.int32)
    code = ids * OWNERS + (block_slot >> 1) + 1
    codes = jnp.sum(jnp.where(place[None, :] == spots[:, None], code[None, :], 0), axis=1)
    last = (first + groups).astype(jnp.int32).reshape(2, 1, POSITIONS)
    anchors = jnp.sum((last <= jnp.arange(MAX_GROUPS, dtype=jnp.int32)[None, :, None]).astype(jnp.int32), axis=2)
    totals = jnp.sum(groups.reshape(2, POSITIONS), axis=1).astype(jnp.int32)
    return codes.reshape(2, -1), anchors, totals, last[0, 0], groups[:POSITIONS].astype(jnp.int32)


def lanes_low(shape):
    return lax.broadcasted_iota(jnp.int32, shape, len(shape) - 1) < KSIZE


def operator_pair(first, second):
    zero = jnp.zeros((KSIZE, 2 * KSIZE), jnp.bfloat16)
    low = lanes_low((KSIZE, 2 * KSIZE))
    turned = [jnp.concatenate([v[:, KSIZE:], v[:, :KSIZE]], axis=1) for v in (first, second)]
    left = jnp.concatenate([
        jnp.where(low, first, zero), jnp.where(low, -turned[0], zero),
        jnp.where(low, zero, turned[1]), jnp.where(low, zero, -second)], axis=0)
    right = jnp.concatenate([
        jnp.where(low, turned[0], zero), jnp.where(low, first, zero),
        jnp.where(low, zero, second), jnp.where(low, zero, turned[1])], axis=0)
    return jnp.concatenate([left, right], axis=1)


def mix_group(code_ref, g, recv, left_of, mixed):
    for pair in range(GROUP // 2):
        picked, rows = [], []
        for i in (2 * pair, 2 * pair + 1):
            code = code_ref[g * GROUP + i]
            place = jnp.maximum(code - 1, 0)
            k = recv[place & (OWNERS - 1)]
            picked.append(jnp.where(code > 0, k, jnp.zeros_like(k)))
            rows.append(left_of(i, place >> 7))
        value = jnp.dot(jnp.concatenate(rows, axis=1), operator_pair(*picked),
                        preferred_element_type=jnp.float32).astype(jnp.bfloat16)
        cols = slice(pair * PATCH, (pair + 1) * PATCH)
        mixed[:PATCH, cols] = value[:, :PATCH]
        mixed[PATCH:, cols] = value[:, PATCH:]


def send_order():
    chips = [(x, y, z) for x in range(4) for y in range(4) for z in range(4)][1:]
    random.Random(0).shuffle(chips)
    order = []
    for chip in chips:
        back = tuple(-d % 4 for d in chip)
        for way in dict.fromkeys((chip, back)):
            if way + (0,) not in order:
                order += [way + (0,), way + (1,)]
    return order + [(0, 0, 0, 1)]


RING = 4


def exchange_kernel(code_ref, anchor_ref, even_hbm, odd_hbm, left_hbm, right_hbm, odd_out, sums_hbm,
                    recv, left, right, mixed, sums, local_sems, send_sems, recv_sems, ring_sems):
    tu, tv = lax.axis_index("tu"), lax.axis_index("tv")
    me = tu * 8 + tv
    x, z, y, core = tu // 4, tu % 4, tv // 2, tv % 2
    for source, target, c in ((even_hbm, recv, 0), (odd_hbm, odd_out, 1)):
        for dx, dy, dz, dc in send_order():
            to_u = (x + dx) % 4 * 4 + (z + dz) % 4
            to_v = (y + dy) % 4 * 2 + (core + dc) % 2
            pltpu.make_async_remote_copy(
                source.at[to_u * 8 + to_v], target.at[me], send_sems.at[c], recv_sems.at[c],
                device_id=(to_u, to_v), device_id_type=pl.DeviceIdType.MESH).start()
    own = [pltpu.make_async_copy(even_hbm.at[me], recv.at[me], local_sems.at[0]),
           pltpu.make_async_copy(odd_hbm.at[me], odd_out.at[me], local_sems.at[1]),
           pltpu.make_async_copy(left_hbm, left, local_sems.at[2]),
           pltpu.make_async_copy(right_hbm, right, local_sems.at[3])]
    for copy in own:
        copy.start()
    mixed[...] = jnp.zeros_like(mixed)
    sums[...] = jnp.zeros_like(sums)
    for copy in own:
        copy.wait()
    others = pl.ds(0, OWNERS - 1)
    pltpu.make_async_copy(recv.at[others], recv.at[others], recv_sems.at[0]).wait()

    def entry(g):
        slot = lax.rem(g, RING)
        return pltpu.make_async_copy(sums.at[slot], sums_hbm.at[g], ring_sems.at[slot])

    def step(g, carry):
        @pl.when(g >= RING)
        def _():
            entry(g - RING).wait()
        before = jnp.maximum(g - 1, 0)
        blocks = [jnp.maximum(code_ref[before * GROUP + i] - 1, 0) >> 7 for i in range(GROUP)]
        weights = jnp.concatenate([right[block] for block in blocks], axis=0)
        patch = jnp.dot(mixed[...], weights, preferred_element_type=jnp.float32)
        mix_group(code_ref, jnp.minimum(g, MAX_GROUPS - 1), recv, lambda i, block: left[block], mixed)
        same = anchor_ref[before] == anchor_ref[jnp.maximum(g - 2, 0)]
        prior = sums[lax.rem(g + RING - 1, RING)]
        sums[lax.rem(g, RING)] = patch + jnp.where(same, prior, jnp.zeros_like(prior))
        entry(g).start()
        return carry
    lax.fori_loop(0, MAX_GROUPS + 1, step, 0)
    for g in range(MAX_GROUPS + 1 - RING, MAX_GROUPS + 1):
        entry(g).wait()
    for c, source, target in ((0, even_hbm, recv), (1, odd_hbm, odd_out)):
        if c:
            pltpu.make_async_copy(target.at[others], target.at[others], recv_sems.at[c]).wait()
        pltpu.make_async_copy(source.at[others], source.at[others], send_sems.at[c]).wait()


def exchange(code, anchor, even, odd, left, right):
    smem = pl.BlockSpec(memory_space=pltpu.SMEM)
    hbm = pl.BlockSpec(memory_space=pltpu.MemorySpace.HBM)
    return pl.pallas_call(
        exchange_kernel,
        out_shape=(jax.ShapeDtypeStruct(odd.shape, odd.dtype),
                   jax.ShapeDtypeStruct((MAX_GROUPS + 1, 2 * PATCH, PATCH), jnp.float32)),
        in_specs=[smem, smem, hbm, hbm, hbm, hbm],
        out_specs=(hbm, hbm),
        scratch_shapes=[
            pltpu.VMEM(even.shape, even.dtype),
            pltpu.VMEM(left.shape, left.dtype),
            pltpu.VMEM(right.shape, right.dtype),
            pltpu.VMEM((2 * PATCH, GROUP * KSIZE), jnp.bfloat16),
            pltpu.VMEM((RING, 2 * PATCH, PATCH), jnp.float32),
            pltpu.SemaphoreType.DMA((4,)),
            pltpu.SemaphoreType.DMA((2,)),
            pltpu.SemaphoreType.DMA((2,)),
            pltpu.SemaphoreType.DMA((RING,)),
        ],
        compiler_params=pltpu.CompilerParams(has_side_effects=True),
        name="exchange",
    )(code, anchor, even, odd, left, right)


def turn(v):
    return pltpu.roll(v, KSIZE, 1)


def finish_kernel(code_ref, anchor_ref, total_ref, end_ref, even_groups, recv_hbm, left_hbm, right_hbm,
                  sums_hbm, main, bottom, side, recv, grid, mixed, lbuf, rbuf, sums, sems, misc_sems):
    total = total_ref[0]
    received = pltpu.make_async_copy(recv_hbm, recv, misc_sems.at[0])
    received.start()

    def copies(g):
        slot = lax.rem(g, DEPTH)
        out = []
        for i in range(GROUP):
            block = jnp.maximum(code_ref[g * GROUP + i] - 1, 0) >> 7
            out.append(pltpu.make_async_copy(left_hbm.at[block], lbuf.at[slot, i], sems.at[slot, i]))
            out.append(pltpu.make_async_copy(
                right_hbm.at[block], rbuf.at[slot, pl.ds(i * KSIZE, KSIZE)], sems.at[slot, GROUP + i]))
        return out

    def start(g):
        for copy in copies(g):
            copy.start()

    for g in range(DEPTH - 2):
        @pl.when(g < total)
        def _():
            start(g)

    def even_sum(q):
        return pltpu.make_async_copy(sums_hbm.at[end_ref[q]], sums.at[q], misc_sems.at[1 + q])

    def start_sum(q, carry):
        @pl.when(even_groups[q] > 0)
        def _():
            even_sum(q).start()
        return carry
    lax.fori_loop(0, POSITIONS, start_sum, 0)
    grid[...] = jnp.zeros_like(grid)
    mixed[...] = jnp.zeros_like(mixed)
    rbuf[DEPTH - 1] = jnp.zeros_like(rbuf[0])
    received.wait()

    def add(anchor, patch):
        row = pl.ds(pl.multiple_of((anchor >> 3) * KSIZE, KSIZE), PATCH)
        odd, col = anchor & 1, (anchor & 7) >> 1
        grid[odd, col, 0, row, :] += patch[:PATCH]
        grid[odd, col, 1, row, :] += patch[PATCH:]

    def step(g, carry):
        @pl.when(g + DEPTH - 2 < total)
        def _():
            start(g + DEPTH - 2)

        @pl.when(g < total)
        def _():
            for copy in copies(g):
                copy.wait()
        patch = jnp.dot(mixed[...], rbuf[lax.rem(g + DEPTH - 1, DEPTH)], preferred_element_type=jnp.float32)
        slot = lax.rem(g, DEPTH)
        mix_group(code_ref, jnp.minimum(g, MAX_GROUPS - 1), recv, lambda i, block: lbuf[slot, i], mixed)
        add(anchor_ref[jnp.maximum(g - 1, 0)], patch)
        return carry

    @pl.when(total > 0)
    def _():
        lax.fori_loop(0, total + 1, step, 0)

    def add_sum(q, carry):
        @pl.when(even_groups[q] > 0)
        def _():
            even_sum(q).wait()
            add(q, sums[q])
        return carry
    lax.fori_loop(0, POSITIONS, add_sum, 0)
    low = lanes_low((KSIZE, PATCH))
    for plane in range(2):
        for r in range(EXT_U // KSIZE):
            rows = slice(r * KSIZE, (r + 1) * KSIZE)
            shifted = [turn(grid[1, col, plane, rows, :]) for col in range(4)]
            for col in range(4):
                before = shifted[col - 1] if col else jnp.zeros_like(shifted[0])
                value = grid[0, col, plane, rows, :] + jnp.where(low, before, shifted[col])
                cols = slice(col * PATCH, (col + 1) * PATCH)
                if r < TILE_U // KSIZE:
                    main[plane, rows, cols] = value
                else:
                    bottom[plane, :, cols] = value.astype(jnp.bfloat16)
    for r in range(EXT_U // KSIZE):
        rows = slice(r * KSIZE, (r + 1) * KSIZE)
        value = jnp.where(low, turn(grid[1, 3, 0, rows, :]), grid[1, 3, 1, rows, :])
        side[rows, :] = value.astype(jnp.bfloat16)


GRID_SHAPE = (2, 4, 2, EXT_U, PATCH)


def finish(code, anchor, total, ends, even_groups, recv, left, right, sums):
    vmem = pl.BlockSpec(memory_space=pltpu.VMEM)
    smem = pl.BlockSpec(memory_space=pltpu.SMEM)
    hbm = pl.BlockSpec(memory_space=pltpu.MemorySpace.HBM)
    return pl.pallas_call(
        finish_kernel,
        out_shape=(jax.ShapeDtypeStruct((2, TILE_U, TILE_V), jnp.float32),
                   jax.ShapeDtypeStruct((2, KSIZE, TILE_V), jnp.bfloat16),
                   jax.ShapeDtypeStruct((EXT_U, PATCH), jnp.bfloat16)),
        in_specs=[smem] * 5 + [hbm] * 4,
        out_specs=(vmem, vmem, vmem),
        scratch_shapes=[
            pltpu.VMEM(recv.shape, recv.dtype),
            pltpu.VMEM(GRID_SHAPE, jnp.float32),
            pltpu.VMEM((2 * PATCH, GROUP * KSIZE), jnp.bfloat16),
            pltpu.VMEM((DEPTH, GROUP, PATCH, 2 * KSIZE), jnp.bfloat16),
            pltpu.VMEM((DEPTH, GROUP * KSIZE, PATCH), jnp.bfloat16),
            pltpu.VMEM((POSITIONS, 2 * PATCH, PATCH), jnp.float32),
            pltpu.SemaphoreType.DMA((DEPTH, 2 * GROUP)),
            pltpu.SemaphoreType.DMA((1 + POSITIONS,)),
        ],
        cost_estimate=pl.CostEstimate(flops=1_000_000_000, bytes_accessed=12_000_000,
                                      transcendentals=0),
        name="finish",
    )(code, anchor, total, ends, even_groups, recv, left, right, sums)


def join_kernel(main, bottom, side, corner, out):
    low = lanes_low((TILE_U, PATCH))
    out[...] = main[...]
    out[:, :KSIZE, :] += bottom[...].astype(jnp.float32)
    edge = side[...].astype(jnp.float32)
    zero = jnp.zeros_like(edge)
    low_corner = lanes_low((KSIZE, PATCH))
    tip = corner[...].astype(jnp.float32)
    out[0, :, :PATCH] += jnp.where(low, edge, zero)
    out[1, :, :PATCH] += jnp.where(low, turn(edge), zero)
    out[0, :KSIZE, :PATCH] += jnp.where(low_corner, tip, zero[:KSIZE])
    out[1, :KSIZE, :PATCH] += jnp.where(low_corner, turn(tip), zero[:KSIZE])


def shards(aperture_amp, aperture_phase, plane_depths, send_list, send_count, vis_left, vis_right,
           block_slot, block_pos, block_count):
    axes = ("tu", "tv")
    n_tu, n_tv = lax.axis_size("tu"), lax.axis_size("tv")
    codes, anchors, totals, ends, even_groups = schedule_blocks(block_slot, block_pos, block_count)
    even, odd = make_outgoing(plane_depths, send_list, aperture_amp, aperture_phase)
    recv, sums = exchange(codes[0], anchors[0], even, odd, vis_left, vis_right)
    main, bottom, side = finish(codes[1], anchors[1], totals[1:], ends, even_groups, recv,
                                vis_left, vis_right, sums)
    bottom = lax.ppermute(bottom, "tu", [(i, i + 1) for i in range(n_tu - 1)])
    corner = lax.ppermute(side[TILE_U:], axes, [
        (u * n_tv + v, (u + 1) * n_tv + v + 1) for u in range(n_tu - 1) for v in range(n_tv - 1)])
    side = lax.ppermute(side[:TILE_U], "tv", [(i, i + 1) for i in range(n_tv - 1)])
    vmem = pl.BlockSpec(memory_space=pltpu.VMEM)
    return pl.pallas_call(
        join_kernel,
        out_shape=jax.ShapeDtypeStruct((2, TILE_U, TILE_V), jnp.float32),
        in_specs=[vmem] * 4,
        out_specs=vmem,
        cost_estimate=pl.CostEstimate(flops=1_000_000, bytes_accessed=2_300_000, transcendentals=0),
        name="join_borders",
    )(main, bottom, side, corner)


def solution(mesh):
    placed = (
        P(("tu", "tv"), None, None),
        P(("tu", "tv"), None, None),
        P(),
        P(("tu", "tv"), None, None),
        P(("tu", "tv"), None),
        P(("tu", "tv"), None, None),
        P(("tu", "tv"), None, None),
        P(("tu", "tv")),
        P(("tu", "tv")),
        P(("tu", "tv")),
    )
    return jax.shard_map(
        shards, mesh=mesh, in_specs=placed, out_specs=P(None, "tu", "tv"), check_vma=False
    )
```

```python
import math
import random

import jax
import jax.numpy as jnp
import numpy as np
from jax import lax
from jax.experimental import pallas as pl
from jax.experimental.pallas import tpu as pltpu
from jax.sharding import PartitionSpec as P

SCREEN = 512
KSIZE = 64
PATCH = 128
PLANES = 4
SCREENS_DEV = 4
BLOCKS_DEV = 384
OWNERS = 128
TILE_U = 256
TILE_V = 512
POSITIONS = 32
GROUP = 4
MAX_GROUPS = BLOCKS_DEV // GROUP + POSITIONS
DEPTH = 6
EXT_U = TILE_U + KSIZE

SIN = (0.9999995827674866, -0.16666553914546967, 0.008332408033311367,
       -0.00019808740762528032, 2.6998227440344635e-06, -2.036623314438657e-08)
COS = (0.9999992251396179, -0.49999427795410156, 0.041659820824861526,
       -0.0013858915772289038, 2.4204400688176975e-05, -2.19788830690959e-07)


def sincos(x):
    z = x * x
    s = jnp.float32(SIN[-1])
    for c in SIN[-2::-1]:
        s = s * z + c
    k = jnp.float32(COS[-1])
    for c in COS[-2::-1]:
        k = k * z + c
    return s * x, k


def dft_rows():
    freq = np.arange(KSIZE) - KSIZE // 2
    turns = np.mod(freq[:, None] * np.arange(SCREEN)[None, :], SCREEN)
    angles = 2.0 * math.pi / SCREEN * turns
    return np.stack([np.cos(angles), -np.sin(angles)]).astype(np.float32)


def screen_kernel(w_hbm, list_ref, amp_hbm, phase_hbm, f_hbm, slot_hbm, pos_hbm, count_hbm,
                  even_hbm, odd_hbm, plan_hbm, even_ref, odd_ref, w_ref, count_ref, slot_ref, pos_ref,
                  plan_ref, f_ref, amp_ref, phase_ref, weight, parts, halves, kernels, sems):
    small = [pltpu.make_async_copy(w_hbm, w_ref, sems.at[0]),
             pltpu.make_async_copy(f_hbm, f_ref, sems.at[1]),
             pltpu.make_async_copy(slot_hbm, slot_ref, sems.at[12]),
             pltpu.make_async_copy(pos_hbm, pos_ref, sems.at[13]),
             pltpu.make_async_copy(count_hbm, count_ref, sems.at[14])]
    loads = [(pltpu.make_async_copy(phase_hbm.at[s], phase_ref.at[s], sems.at[2 + 2 * s]),
              pltpu.make_async_copy(amp_hbm.at[s], amp_ref.at[s], sems.at[3 + 2 * s]))
             for s in range(SCREENS_DEV)]
    for copy in small + [c for pair in loads for c in pair]:
        copy.start()
    for copy in small:
        copy.wait()
    coords = (lax.broadcasted_iota(jnp.int32, (1, SCREEN), 1) - SCREEN // 2).astype(jnp.float32)
    square = coords * coords * (1.0 / (SCREEN * SCREEN))
    for p in range(PLANES):
        turns = square * w_ref[p]
        turns = turns - jnp.floor(turns + 0.5)
        sin_p, cos_p = sincos(turns * (2.0 * math.pi))
        f_re, f_im = f_ref[0], f_ref[1]
        w_re = (f_re * cos_p - f_im * sin_p).astype(jnp.bfloat16)
        w_im = (f_re * sin_p + f_im * cos_p).astype(jnp.bfloat16)
        top = slice(p * 2 * KSIZE, p * 2 * KSIZE + KSIZE)
        low = slice(p * 2 * KSIZE + KSIZE, (p + 1) * 2 * KSIZE)
        weight[top, :SCREEN] = w_re
        weight[top, SCREEN:] = -w_im
        weight[low, :SCREEN] = w_im
        weight[low, SCREEN:] = w_re
    rows = 32
    for s in range(SCREENS_DEV):
        for copy in loads[s]:
            copy.wait()

        def fill(i, carry):
            at = pl.ds(pl.multiple_of(i * rows, rows), rows)
            sin_v, cos_v = sincos(phase_ref[s, at, :].astype(jnp.float32))
            amp = amp_ref[s, at, :].astype(jnp.float32)
            parts[s % 2, at, :] = (amp * cos_v).astype(jnp.bfloat16)
            parts[s % 2, pl.ds(pl.multiple_of(SCREEN + i * rows, rows), rows), :] = (
                amp * sin_v).astype(jnp.bfloat16)
            return carry
        lax.fori_loop(0, SCREEN // rows, fill, 0)
        for p in range(PLANES):
            half = jnp.dot(weight[p * 128:(p + 1) * 128, :], parts[s % 2],
                           preferred_element_type=jnp.float32).astype(jnp.bfloat16)
            halves[p, s * KSIZE:(s + 1) * KSIZE, :SCREEN] = half[:KSIZE]
            halves[p, s * KSIZE:(s + 1) * KSIZE, SCREEN:] = half[KSIZE:]
    for p in range(PLANES):
        out = lax.dot_general(halves[p], weight[p * 128:(p + 1) * 128, :],
                              (((1,), (1,)), ((), ())), preferred_element_type=jnp.float32)
        out = (out * (1.0 / SCREEN)).astype(jnp.bfloat16)
        for s in range(SCREENS_DEV):
            kernels[s * PLANES + p] = out[s * KSIZE:(s + 1) * KSIZE]

    outs = [pltpu.make_async_copy(plan_ref, plan_hbm, sems.at[15])]
    plan_ref[...] = plan_blocks(slot_ref[...], pos_ref[...], count_ref[0])
    outs[0].start()
    for c, (slots, out) in enumerate([(even_ref, even_hbm), (odd_ref, odd_hbm)]):
        def deliver(t, carry):
            slots[t] = kernels[list_ref[c, t]]
            return carry
        lax.fori_loop(0, OWNERS, deliver, 0)
        outs.append(pltpu.make_async_copy(slots, out, sems.at[10 + c]))
        outs[-1].start()
    for copy in outs:
        copy.wait()


def make_outgoing(depths, send_list, amp, phase, block_slot, block_pos, block_count):
    smem = pl.BlockSpec(memory_space=pltpu.SMEM)
    hbm = pl.BlockSpec(memory_space=pltpu.MemorySpace.HBM)
    slots = jax.ShapeDtypeStruct((OWNERS, KSIZE, 2 * KSIZE), jnp.bfloat16)
    return pl.pallas_call(
        screen_kernel,
        out_shape=(slots, slots, jax.ShapeDtypeStruct((16, 128), jnp.int32)),
        in_specs=[hbm, smem] + [hbm] * 6,
        out_specs=(hbm,) * 3,
        scratch_shapes=[
            pltpu.VMEM(slots.shape, slots.dtype),
            pltpu.VMEM(slots.shape, slots.dtype),
            pltpu.SMEM((PLANES,), jnp.float32),
            pltpu.SMEM((1,), jnp.int32),
            pltpu.VMEM((3, 128), jnp.int32),
            pltpu.VMEM((3, 128), jnp.int32),
            pltpu.VMEM((16, 128), jnp.int32),
            pltpu.VMEM((2, KSIZE, SCREEN), jnp.float32),
            pltpu.VMEM((SCREENS_DEV, SCREEN, SCREEN), jnp.bfloat16),
            pltpu.VMEM((SCREENS_DEV, SCREEN, SCREEN), jnp.bfloat16),
            pltpu.VMEM((PLANES * 128, 2 * SCREEN), jnp.bfloat16),
            pltpu.VMEM((2, 2 * SCREEN, SCREEN), jnp.bfloat16),
            pltpu.VMEM((PLANES, SCREENS_DEV * KSIZE, 2 * SCREEN), jnp.bfloat16),
            pltpu.VMEM((SCREENS_DEV * PLANES, KSIZE, 2 * KSIZE), jnp.bfloat16),
            pltpu.SemaphoreType.DMA((16,)),
        ],
        cost_estimate=pl.CostEstimate(flops=2_700_000_000, bytes_accessed=8_600_000,
                                      transcendentals=2_000_000),
        name="screens",
    )(depths, send_list[0].T, amp, phase, jnp.asarray(dft_rows()), block_slot.reshape(3, 128),
      block_pos.reshape(3, 128), block_count)


def iota(shape, dim):
    return lax.broadcasted_iota(jnp.int32, shape, dim)


def plan_blocks(slot, pos, count):
    bins_total = 2 * POSITIONS
    slot, pos = (jnp.concatenate([v[r:r + 1] for r in range(3)], axis=1) for v in (slot, pos))
    ids = iota((1, BLOCKS_DEV), 1)
    parity = slot & 1
    used = ids < count
    bins = jnp.where(used, parity * POSITIONS + pos, -1)
    hot = (iota((bins_total, BLOCKS_DEV), 0) == bins).astype(jnp.float32)
    upto = (iota((BLOCKS_DEV, BLOCKS_DEV), 0) <= iota((BLOCKS_DEV, BLOCKS_DEV), 1)).astype(jnp.float32)
    count_to = jnp.dot(hot.astype(jnp.bfloat16), upto.astype(jnp.bfloat16),
                       preferred_element_type=jnp.float32)
    rank = jnp.sum(count_to * hot, axis=0, keepdims=True) - 1.0
    groups = jnp.floor((jnp.sum(hot, axis=1, keepdims=True) + (GROUP - 1.0)) * (1.0 / GROUP))
    wide = jnp.broadcast_to(groups, (bins_total, 128))
    b_row, b_col = iota((bins_total, bins_total), 0), iota((bins_total, bins_total), 1)
    earlier = ((b_col < b_row) & ((b_col >= POSITIONS) == (b_row >= POSITIONS))).astype(jnp.float32)
    first = jnp.dot(earlier.astype(jnp.bfloat16), wide.astype(jnp.bfloat16),
                    preferred_element_type=jnp.float32)
    last = first + wide
    place = jnp.sum(hot * first[:, :1], axis=0, keepdims=True) * GROUP + rank
    place = jnp.where(used, place.astype(jnp.int32) + parity * (MAX_GROUPS * GROUP), -1)
    high = (iota((8, BLOCKS_DEV), 0) == (place >> 7)).astype(jnp.float32)
    low = (iota((128, BLOCKS_DEV), 0) == (place & 127)).astype(jnp.float32)
    parts = [(slot >> 1).astype(jnp.float32), (ids & 127).astype(jnp.float32),
             ((ids >> 7) + 1).astype(jnp.float32)]
    spread = lax.dot_general(
        jnp.concatenate([high * part for part in parts], axis=0).astype(jnp.bfloat16),
        low.astype(jnp.bfloat16), (((1,), (1,)), ((), ())), preferred_element_type=jnp.float32)
    owner, block_low, block_high = spread[:8], spread[8:16], spread[16:]
    codes = jnp.where(block_high > 0.0,
                      ((block_high - 1.0) * 128.0 + block_low) * OWNERS + owner + 1.0, 0.0)
    lanes = iota((bins_total, 128), 1)
    past = (last <= lanes.astype(jnp.float32)).astype(jnp.float32)
    onto = (iota((bins_total, 128), 0) == lanes).astype(jnp.float32)
    rows = [codes, jnp.sum(past[:POSITIONS], axis=0, keepdims=True),
            jnp.sum(past[POSITIONS:], axis=0, keepdims=True),
            jnp.sum(onto * last, axis=0, keepdims=True),
            jnp.sum(onto * wide, axis=0, keepdims=True),
            jnp.sum(wide[:POSITIONS], axis=0, keepdims=True),
            jnp.sum(wide[POSITIONS:], axis=0, keepdims=True),
            jnp.zeros((2, 128), jnp.float32)]
    return jnp.concatenate(rows, axis=0).astype(jnp.int32)


ANCHOR_ROW, END_ROW, GROUPS_ROW, TOTAL_ROW = 8, 10, 11, 12


def entry_code(plan, parity, g, i):
    return plan[parity * 4 + (g >> 5), (g & 31) * GROUP + i]


def lanes_low(shape):
    return lax.broadcasted_iota(jnp.int32, shape, len(shape) - 1) < KSIZE


def operator_pair(first, second):
    zero = jnp.zeros((KSIZE, 2 * KSIZE), jnp.bfloat16)
    low = lanes_low((KSIZE, 2 * KSIZE))
    turned = [jnp.concatenate([v[:, KSIZE:], v[:, :KSIZE]], axis=1) for v in (first, second)]
    left = jnp.concatenate([
        jnp.where(low, first, zero), jnp.where(low, -turned[0], zero),
        jnp.where(low, zero, turned[1]), jnp.where(low, zero, -second)], axis=0)
    right = jnp.concatenate([
        jnp.where(low, turned[0], zero), jnp.where(low, first, zero),
        jnp.where(low, zero, second), jnp.where(low, zero, turned[1])], axis=0)
    return jnp.concatenate([left, right], axis=1)


def mix_group(plan, parity, g, recv, left_of, mixed):
    for pair in range(GROUP // 2):
        picked, rows = [], []
        for i in (2 * pair, 2 * pair + 1):
            code = entry_code(plan, parity, g, i)
            place = jnp.maximum(code - 1, 0)
            k = recv[place & (OWNERS - 1)]
            picked.append(jnp.where(code > 0, k, jnp.zeros_like(k)))
            rows.append(left_of(i, place >> 7))
        value = jnp.dot(jnp.concatenate(rows, axis=1), operator_pair(*picked),
                        preferred_element_type=jnp.float32).astype(jnp.bfloat16)
        cols = slice(pair * PATCH, (pair + 1) * PATCH)
        mixed[:PATCH, cols] = value[:, :PATCH]
        mixed[PATCH:, cols] = value[:, PATCH:]


def send_order():
    chips = [(x, y, z) for x in range(4) for y in range(4) for z in range(4)][1:]
    random.Random(0).shuffle(chips)
    order = []
    for chip in chips:
        back = tuple(-d % 4 for d in chip)
        for way in dict.fromkeys((chip, back)):
            if way + (0,) not in order:
                order += [way + (0,), way + (1,)]
    return order + [(0, 0, 0, 1)]


RING = 4
UNROLL = 2
STEPS = MAX_GROUPS // UNROLL + 1


def exchange_kernel(plan, even_hbm, odd_hbm, left_hbm, right_hbm, odd_out, sums_hbm,
                    recv, left, right, mixed, sums, local_sems, send_sems, recv_sems, ring_sems):
    tu, tv = lax.axis_index("tu"), lax.axis_index("tv")
    me = tu * 8 + tv
    x, z, y, core = tu // 4, tu % 4, tv // 2, tv % 2
    for source, target, c in ((even_hbm, recv, 0), (odd_hbm, odd_out, 1)):
        for dx, dy, dz, dc in send_order():
            to_u = (x + dx) % 4 * 4 + (z + dz) % 4
            to_v = (y + dy) % 4 * 2 + (core + dc) % 2
            pltpu.make_async_remote_copy(
                source.at[to_u * 8 + to_v], target.at[me], send_sems.at[c], recv_sems.at[c],
                device_id=(to_u, to_v), device_id_type=pl.DeviceIdType.MESH).start()
    own = [pltpu.make_async_copy(even_hbm.at[me], recv.at[me], local_sems.at[0]),
           pltpu.make_async_copy(odd_hbm.at[me], odd_out.at[me], local_sems.at[1]),
           pltpu.make_async_copy(left_hbm, left, local_sems.at[2]),
           pltpu.make_async_copy(right_hbm, right, local_sems.at[3])]
    for copy in own:
        copy.start()
    mixed[...] = jnp.zeros_like(mixed)
    sums[...] = jnp.zeros_like(sums)
    for copy in own:
        copy.wait()
    others = pl.ds(0, OWNERS - 1)
    pltpu.make_async_copy(recv.at[others], recv.at[others], recv_sems.at[0]).wait()

    def entry(h):
        slot = lax.rem(h, RING)
        return pltpu.make_async_copy(sums.at[slot], sums_hbm.at[h], ring_sems.at[slot])

    def step(h, carry):
        @pl.when(h >= RING)
        def _():
            entry(h - RING).wait()
        slot = lax.rem(h, RING)
        patches = []
        for k in range(UNROLL):
            g = jnp.maximum((h - 1) * UNROLL + k, 0)
            blocks = [jnp.maximum(entry_code(plan, 0, g, i) - 1, 0) >> 7 for i in range(GROUP)]
            weights = jnp.concatenate([right[block] for block in blocks], axis=0)
            patches.append(jnp.dot(mixed[k], weights, preferred_element_type=jnp.float32))
        for k in range(UNROLL):
            g = jnp.minimum(h * UNROLL + k, MAX_GROUPS - 1)
            mix_group(plan, 0, g, recv, lambda i, block: left[block], mixed.at[k])
        prior = sums[lax.rem(h + RING - 1, RING), UNROLL - 1]
        for k in range(UNROLL):
            g = jnp.maximum((h - 1) * UNROLL + k, 0)
            same = plan[ANCHOR_ROW, g] == plan[ANCHOR_ROW, jnp.maximum(g - 1, 0)]
            prior = patches[k] + jnp.where(same, prior, jnp.zeros_like(prior))
            sums[slot, k] = prior
        entry(h).start()
        return carry
    lax.fori_loop(0, STEPS, step, 0)
    for h in range(STEPS - RING, STEPS):
        entry(h).wait()
    for c, source, target in ((0, even_hbm, recv), (1, odd_hbm, odd_out)):
        if c:
            pltpu.make_async_copy(target.at[others], target.at[others], recv_sems.at[c]).wait()
        pltpu.make_async_copy(source.at[others], source.at[others], send_sems.at[c]).wait()


def exchange(plan, even, odd, left, right):
    smem = pl.BlockSpec(memory_space=pltpu.SMEM)
    hbm = pl.BlockSpec(memory_space=pltpu.MemorySpace.HBM)
    return pl.pallas_call(
        exchange_kernel,
        out_shape=(jax.ShapeDtypeStruct(odd.shape, odd.dtype),
                   jax.ShapeDtypeStruct((STEPS, UNROLL, 2 * PATCH, PATCH), jnp.float32)),
        in_specs=[smem, hbm, hbm, hbm, hbm],
        out_specs=(hbm, hbm),
        scratch_shapes=[
            pltpu.VMEM(even.shape, even.dtype),
            pltpu.VMEM(left.shape, left.dtype),
            pltpu.VMEM(right.shape, right.dtype),
            pltpu.VMEM((UNROLL, 2 * PATCH, GROUP * KSIZE), jnp.bfloat16),
            pltpu.VMEM((RING, UNROLL, 2 * PATCH, PATCH), jnp.float32),
            pltpu.SemaphoreType.DMA((4,)),
            pltpu.SemaphoreType.DMA((2,)),
            pltpu.SemaphoreType.DMA((2,)),
            pltpu.SemaphoreType.DMA((RING,)),
        ],
        compiler_params=pltpu.CompilerParams(has_side_effects=True),
        name="exchange",
    )(plan, even, odd, left, right)


def turn(v):
    return pltpu.roll(v, KSIZE, 1)


def finish_kernel(plan, recv_hbm, left_hbm, right_hbm, sums_hbm, main, bottom, side,
                  recv, grid, mixed, lbuf, rbuf, sums, sems, misc_sems):
    steps = (plan[TOTAL_ROW + 1, 0] + UNROLL - 1) // UNROLL
    received = pltpu.make_async_copy(recv_hbm, recv, misc_sems.at[0])
    received.start()

    def start(h):
        slot = lax.rem(h, DEPTH)
        for k in range(UNROLL):
            for i in range(GROUP):
                block = jnp.maximum(entry_code(plan, 1, h * UNROLL + k, i) - 1, 0) >> 7
                n = k * GROUP + i
                pltpu.make_async_copy(left_hbm.at[block], lbuf.at[slot, n], sems.at[0, slot]).start()
                pltpu.make_async_copy(right_hbm.at[block], rbuf.at[slot, n], sems.at[1, slot]).start()

    for h in range(DEPTH - 2):
        @pl.when(h < steps)
        def _():
            start(h)

    def even_sum(q):
        at = plan[END_ROW, q] - 1 + UNROLL
        return pltpu.make_async_copy(sums_hbm.at[at // UNROLL, lax.rem(at, UNROLL)], sums.at[q],
                                     misc_sems.at[1 + q])

    def start_sum(q, carry):
        @pl.when(plan[GROUPS_ROW, q] > 0)
        def _():
            even_sum(q).start()
        return carry
    lax.fori_loop(0, POSITIONS, start_sum, 0)
    grid[...] = jnp.zeros_like(grid)
    mixed[...] = jnp.zeros_like(mixed)
    rbuf[DEPTH - 1] = jnp.zeros_like(rbuf[0])
    received.wait()

    def add(anchor, patch):
        row = pl.ds(pl.multiple_of((anchor >> 3) * KSIZE, KSIZE), PATCH)
        odd, col = anchor & 1, (anchor & 7) >> 1
        grid[odd, col, 0, row, :] += patch[:PATCH]
        grid[odd, col, 1, row, :] += patch[PATCH:]

    def step(h, carry):
        slot = lax.rem(h, DEPTH)

        @pl.when(h + DEPTH - 2 < steps)
        def _():
            start(h + DEPTH - 2)

        @pl.when(h < steps)
        def _():
            pltpu.make_async_copy(lbuf.at[slot], lbuf.at[slot], sems.at[0, slot]).wait()
            pltpu.make_async_copy(rbuf.at[slot], rbuf.at[slot], sems.at[1, slot]).wait()
        earlier = lax.rem(h + DEPTH - 1, DEPTH)
        patches = []
        for k in range(UNROLL):
            weights = jnp.concatenate([rbuf[earlier, k * GROUP + i] for i in range(GROUP)], axis=0)
            patches.append(jnp.dot(mixed[k], weights, preferred_element_type=jnp.float32))
        for k in range(UNROLL):
            g = jnp.minimum(h * UNROLL + k, MAX_GROUPS - 1)
            mix_group(plan, 1, g, recv, lambda i, block: lbuf[slot, k * GROUP + i], mixed.at[k])
        for k in range(UNROLL):
            g = jnp.maximum((h - 1) * UNROLL + k, 0)
            add(jnp.minimum(plan[ANCHOR_ROW + 1, g], POSITIONS - 1), patches[k])
        return carry

    @pl.when(steps > 0)
    def _():
        lax.fori_loop(0, steps + 1, step, 0)

    def add_sum(q, carry):
        @pl.when(plan[GROUPS_ROW, q] > 0)
        def _():
            even_sum(q).wait()
            add(q, sums[q])
        return carry
    lax.fori_loop(0, POSITIONS, add_sum, 0)
    low = lanes_low((KSIZE, PATCH))
    for plane in range(2):
        for r in range(EXT_U // KSIZE):
            rows = slice(r * KSIZE, (r + 1) * KSIZE)
            shifted = [turn(grid[1, col, plane, rows, :]) for col in range(4)]
            for col in range(4):
                before = shifted[col - 1] if col else jnp.zeros_like(shifted[0])
                value = grid[0, col, plane, rows, :] + jnp.where(low, before, shifted[col])
                cols = slice(col * PATCH, (col + 1) * PATCH)
                if r < TILE_U // KSIZE:
                    main[plane, rows, cols] = value
                else:
                    bottom[plane, :, cols] = value.astype(jnp.bfloat16)
    for r in range(EXT_U // KSIZE):
        rows = slice(r * KSIZE, (r + 1) * KSIZE)
        value = jnp.where(low, turn(grid[1, 3, 0, rows, :]), grid[1, 3, 1, rows, :])
        side[rows, :] = value.astype(jnp.bfloat16)


GRID_SHAPE = (2, 4, 2, EXT_U, PATCH)


def finish(plan, recv, left, right, sums):
    vmem = pl.BlockSpec(memory_space=pltpu.VMEM)
    smem = pl.BlockSpec(memory_space=pltpu.SMEM)
    hbm = pl.BlockSpec(memory_space=pltpu.MemorySpace.HBM)
    return pl.pallas_call(
        finish_kernel,
        out_shape=(jax.ShapeDtypeStruct((2, TILE_U, TILE_V), jnp.float32),
                   jax.ShapeDtypeStruct((2, KSIZE, TILE_V), jnp.bfloat16),
                   jax.ShapeDtypeStruct((EXT_U, PATCH), jnp.bfloat16)),
        in_specs=[smem] + [hbm] * 4,
        out_specs=(vmem, vmem, vmem),
        scratch_shapes=[
            pltpu.VMEM(recv.shape, recv.dtype),
            pltpu.VMEM(GRID_SHAPE, jnp.float32),
            pltpu.VMEM((UNROLL, 2 * PATCH, GROUP * KSIZE), jnp.bfloat16),
            pltpu.VMEM((DEPTH, UNROLL * GROUP, PATCH, 2 * KSIZE), jnp.bfloat16),
            pltpu.VMEM((DEPTH, UNROLL * GROUP, KSIZE, PATCH), jnp.bfloat16),
            pltpu.VMEM((POSITIONS, 2 * PATCH, PATCH), jnp.float32),
            pltpu.SemaphoreType.DMA((2, DEPTH)),
            pltpu.SemaphoreType.DMA((1 + POSITIONS,)),
        ],
        cost_estimate=pl.CostEstimate(flops=1_000_000_000, bytes_accessed=12_000_000,
                                      transcendentals=0),
        name="finish",
    )(plan, recv, left, right, sums)


def border_kernel(bottom, side, bottom_out, side_out, corner_out, send_sems, recv_sems):
    tu, tv = lax.axis_index("tu"), lax.axis_index("tv")
    n_tu, n_tv = lax.axis_size("tu"), lax.axis_size("tv")
    ways = ((1, 0), (0, 1), (1, 1))
    barrier = pltpu.get_barrier_semaphore()
    for du, dv in ways:
        for sign in (1, -1):
            other = ((tu + n_tu + sign * du) % n_tu, (tv + n_tv + sign * dv) % n_tv)
            pl.semaphore_signal(barrier, inc=1, device_id=other, device_id_type=pl.DeviceIdType.MESH)
    pl.semaphore_wait(barrier, 2 * len(ways))
    parts = ((bottom, bottom_out), (side.at[pl.ds(0, TILE_U)], side_out),
             (side.at[pl.ds(TILE_U, KSIZE)], corner_out))
    copies = []
    for n, ((du, dv), (source, target)) in enumerate(zip(ways, parts)):
        copies.append(pltpu.make_async_remote_copy(
            source, target, send_sems.at[n], recv_sems.at[n],
            device_id=((tu + du) % n_tu, (tv + dv) % n_tv), device_id_type=pl.DeviceIdType.MESH))
        copies[-1].start()
    for copy in copies:
        copy.wait()


def borders(bottom, side):
    hbm = pl.BlockSpec(memory_space=pltpu.MemorySpace.HBM)
    return pl.pallas_call(
        border_kernel,
        out_shape=(jax.ShapeDtypeStruct(bottom.shape, bottom.dtype),
                   jax.ShapeDtypeStruct((TILE_U, PATCH), side.dtype),
                   jax.ShapeDtypeStruct((KSIZE, PATCH), side.dtype)),
        in_specs=[hbm, hbm],
        out_specs=(hbm,) * 3,
        scratch_shapes=[pltpu.SemaphoreType.DMA((3,)), pltpu.SemaphoreType.DMA((3,))],
        compiler_params=pltpu.CompilerParams(collective_id=1, has_side_effects=True),
        name="borders",
    )(bottom, side)


def join_kernel(main, bottom_hbm, side_hbm, corner_hbm, out, top, left, bottom, side, corner, sems):
    strips = [(top, (slice(None), pl.ds(0, KSIZE))),
              (left, (slice(None), pl.ds(KSIZE, TILE_U - KSIZE), pl.ds(0, PATCH)))]
    loads = [pltpu.make_async_copy(main.at[at], strip, sems.at[n]) for n, (strip, at) in enumerate(strips)]
    loads += [pltpu.make_async_copy(bottom_hbm, bottom, sems.at[2]),
              pltpu.make_async_copy(side_hbm, side, sems.at[3]),
              pltpu.make_async_copy(corner_hbm, corner, sems.at[4])]
    for copy in loads:
        copy.start()
    for copy in loads:
        copy.wait()
    above, beside = lax.axis_index("tu") > 0, lax.axis_index("tv") > 0

    def kept(flag, value):
        value = value.astype(jnp.float32)
        return jnp.where(flag, value, jnp.zeros_like(value))
    top[...] += kept(above, bottom[...])
    edge = kept(beside, side[...])
    tip = kept(above & beside, corner[...]) + edge[:KSIZE]
    low = lanes_low((KSIZE, PATCH))
    zero = jnp.zeros((KSIZE, PATCH), jnp.float32)
    top[0, :, :PATCH] += jnp.where(low, tip, zero)
    top[1, :, :PATCH] += jnp.where(low, turn(tip), zero)
    for r in range(1, TILE_U // KSIZE):
        rows = slice((r - 1) * KSIZE, r * KSIZE)
        part = edge[r * KSIZE:(r + 1) * KSIZE]
        left[0, rows, :] += jnp.where(low, part, zero)
        left[1, rows, :] += jnp.where(low, turn(part), zero)
    stores = [pltpu.make_async_copy(strip, out.at[at], sems.at[5 + n]) for n, (strip, at) in enumerate(strips)]
    for copy in stores:
        copy.start()
    for copy in stores:
        copy.wait()


def join(main, bottom, side, corner):
    hbm = pl.BlockSpec(memory_space=pltpu.MemorySpace.HBM)
    return pl.pallas_call(
        join_kernel,
        out_shape=jax.ShapeDtypeStruct(main.shape, main.dtype),
        in_specs=[hbm] * 4,
        out_specs=hbm,
        input_output_aliases={0: 0},
        scratch_shapes=[
            pltpu.VMEM((2, KSIZE, TILE_V), jnp.float32),
            pltpu.VMEM((2, TILE_U - KSIZE, PATCH), jnp.float32),
            pltpu.VMEM(bottom.shape, bottom.dtype),
            pltpu.VMEM(side.shape, side.dtype),
            pltpu.VMEM(corner.shape, corner.dtype),
            pltpu.SemaphoreType.DMA((7,)),
        ],
        name="join_borders",
    )(main, bottom, side, corner)


def shards(aperture_amp, aperture_phase, plane_depths, send_list, send_count, vis_left, vis_right,
           block_slot, block_pos, block_count):
    even, odd, plan = make_outgoing(plane_depths, send_list, aperture_amp, aperture_phase,
                                    block_slot, block_pos, block_count)
    recv, sums = exchange(plan, even, odd, vis_left, vis_right)
    main, bottom, side = finish(plan, recv, vis_left, vis_right, sums)
    return join(main, *borders(bottom, side))


def solution(mesh):
    placed = (
        P(("tu", "tv"), None, None),
        P(("tu", "tv"), None, None),
        P(),
        P(("tu", "tv"), None, None),
        P(("tu", "tv"), None),
        P(("tu", "tv"), None, None),
        P(("tu", "tv"), None, None),
        P(("tu", "tv")),
        P(("tu", "tv")),
        P(("tu", "tv")),
    )
    return jax.shard_map(
        shards, mesh=mesh, in_specs=placed, out_specs=P(None, "tu", "tv"), check_vma=False
    )
```

```python
import math
import random

import jax
import jax.numpy as jnp
import numpy as np
from jax import lax
from jax.experimental import pallas as pl
from jax.experimental.pallas import tpu as pltpu
from jax.sharding import PartitionSpec as P

SCREEN = 512
KSIZE = 64
PATCH = 128
PLANES = 4
SCREENS_DEV = 4
BLOCKS_DEV = 384
OWNERS = 128
TILE_U = 256
TILE_V = 512
POSITIONS = 32
GROUP = 4
MAX_GROUPS = BLOCKS_DEV // GROUP + POSITIONS
DEPTH = 6
EXT_U = TILE_U + KSIZE

SIN = (0.9999995827674866, -0.16666553914546967, 0.008332408033311367,
       -0.00019808740762528032, 2.6998227440344635e-06, -2.036623314438657e-08)
COS = (0.9999992251396179, -0.49999427795410156, 0.041659820824861526,
       -0.0013858915772289038, 2.4204400688176975e-05, -2.19788830690959e-07)


def sincos(x):
    z = x * x
    s = jnp.float32(SIN[-1])
    for c in SIN[-2::-1]:
        s = s * z + c
    k = jnp.float32(COS[-1])
    for c in COS[-2::-1]:
        k = k * z + c
    return s * x, k


HALF_SIN = (0.7071043848991394, -0.029459532350301743, 0.0003670911828521639, -2.0289162421249785e-06)
HALF_COS = (1.4142135381698608, -0.17677636444568634, 0.003682575421407819, -3.061264942516573e-05,
            1.279086063732393e-07)


def polar(amp, x):
    z = x * x
    s = jnp.float32(HALF_SIN[-1])
    for c in HALF_SIN[-2::-1]:
        s = s * z + c
    s = s * x
    k = jnp.float32(HALF_COS[-1])
    for c in HALF_COS[-2::-1]:
        k = k * z + c
    scaled = amp * s
    return amp - scaled * s, scaled * k


def dft_rows():
    freq = np.arange(KSIZE) - KSIZE // 2
    turns = np.mod(freq[:, None] * np.arange(SCREEN)[None, :], SCREEN)
    angles = 2.0 * math.pi / SCREEN * turns
    return np.stack([np.cos(angles), -np.sin(angles)]).astype(np.float32)


def screen_kernel(w_hbm, list_ref, amp_hbm, phase_hbm, f_hbm, slot_hbm, pos_hbm, count_hbm,
                  even_hbm, odd_hbm, plan_hbm, even_ref, odd_ref, w_ref, count_ref, slot_ref, pos_ref,
                  plan_ref, f_ref, amp_ref, phase_ref, weight, parts_a, parts_b, halves, kernels, sems):
    small = [pltpu.make_async_copy(w_hbm, w_ref, sems.at[0]),
             pltpu.make_async_copy(f_hbm, f_ref, sems.at[1]),
             pltpu.make_async_copy(slot_hbm, slot_ref, sems.at[12]),
             pltpu.make_async_copy(pos_hbm, pos_ref, sems.at[13]),
             pltpu.make_async_copy(count_hbm, count_ref, sems.at[14])]
    loads = [(pltpu.make_async_copy(phase_hbm.at[s], phase_ref.at[s], sems.at[2 + 2 * s]),
              pltpu.make_async_copy(amp_hbm.at[s], amp_ref.at[s], sems.at[3 + 2 * s]))
             for s in range(SCREENS_DEV)]
    for copy in small + [c for pair in loads for c in pair]:
        copy.start()
    for copy in small:
        copy.wait()
    coords = (lax.broadcasted_iota(jnp.int32, (1, SCREEN), 1) - SCREEN // 2).astype(jnp.float32)
    square = coords * coords * (1.0 / (SCREEN * SCREEN))
    for p in range(PLANES):
        turns = square * w_ref[p]
        turns = turns - jnp.floor(turns + 0.5)
        sin_p, cos_p = sincos(turns * (2.0 * math.pi))
        f_re, f_im = f_ref[0], f_ref[1]
        w_re = (f_re * cos_p - f_im * sin_p).astype(jnp.bfloat16)
        w_im = (f_re * sin_p + f_im * cos_p).astype(jnp.bfloat16)
        top = slice(p * 2 * KSIZE, p * 2 * KSIZE + KSIZE)
        low = slice(p * 2 * KSIZE + KSIZE, (p + 1) * 2 * KSIZE)
        weight[top, :SCREEN] = w_re
        weight[top, SCREEN:] = -w_im
        weight[low, :SCREEN] = w_im
        weight[low, SCREEN:] = w_re
    rows = 16
    parts = (parts_a, parts_b)
    for s in range(SCREENS_DEV + 1):
        if s < SCREENS_DEV:
            for copy in loads[s]:
                copy.wait()

        def part(p, carry):
            if s > 0:
                at = pl.ds(pl.multiple_of(p * 128, 128), 128)
                half = jnp.dot(weight[at, :], parts[(s - 1) % 2][...], preferred_element_type=jnp.float32)
                half = half.astype(jnp.bfloat16)
                kept = slice((s - 1) * KSIZE, s * KSIZE)
                halves[p, kept, :SCREEN] = half[:KSIZE]
                halves[p, kept, SCREEN:] = half[KSIZE:]
            if s < SCREENS_DEV:
                for i in range(SCREEN // PLANES // rows):
                    start = pl.multiple_of(p * (SCREEN // PLANES) + i * rows, rows)
                    at = pl.ds(start, rows)
                    re, im = polar(amp_ref[s, at, :].astype(jnp.float32), phase_ref[s, at, :].astype(jnp.float32))
                    parts[s % 2][at, :] = re.astype(jnp.bfloat16)
                    parts[s % 2][pl.ds(pl.multiple_of(SCREEN + start, rows), rows), :] = im.astype(jnp.bfloat16)
            return carry
        lax.fori_loop(0, PLANES, part, 0)
    for p in range(PLANES):
        out = lax.dot_general(halves[p], weight[p * 128:(p + 1) * 128, :],
                              (((1,), (1,)), ((), ())), preferred_element_type=jnp.float32)
        out = (out * (1.0 / SCREEN)).astype(jnp.bfloat16)
        for s in range(SCREENS_DEV):
            kernels[s * PLANES + p] = out[s * KSIZE:(s + 1) * KSIZE]

    outs = [pltpu.make_async_copy(plan_ref, plan_hbm, sems.at[15])]
    plan_ref[...] = plan_blocks(slot_ref[...], pos_ref[...], count_ref[0])
    outs[0].start()
    for c, (slots, out) in enumerate([(even_ref, even_hbm), (odd_ref, odd_hbm)]):
        def deliver(t, carry):
            slots[t] = kernels[list_ref[c, t]]
            return carry
        lax.fori_loop(0, OWNERS, deliver, 0)
        outs.append(pltpu.make_async_copy(slots, out, sems.at[10 + c]))
        outs[-1].start()
    for copy in outs:
        copy.wait()


def make_outgoing(depths, send_list, amp, phase, block_slot, block_pos, block_count):
    smem = pl.BlockSpec(memory_space=pltpu.SMEM)
    hbm = pl.BlockSpec(memory_space=pltpu.MemorySpace.HBM)
    slots = jax.ShapeDtypeStruct((OWNERS, KSIZE, 2 * KSIZE), jnp.bfloat16)
    return pl.pallas_call(
        screen_kernel,
        out_shape=(slots, slots, jax.ShapeDtypeStruct((PLAN_ROWS, 128), jnp.int32)),
        in_specs=[hbm, smem] + [hbm] * 6,
        out_specs=(hbm,) * 3,
        scratch_shapes=[
            pltpu.VMEM(slots.shape, slots.dtype),
            pltpu.VMEM(slots.shape, slots.dtype),
            pltpu.SMEM((PLANES,), jnp.float32),
            pltpu.SMEM((1,), jnp.int32),
            pltpu.VMEM((3, 128), jnp.int32),
            pltpu.VMEM((3, 128), jnp.int32),
            pltpu.VMEM((PLAN_ROWS, 128), jnp.int32),
            pltpu.VMEM((2, KSIZE, SCREEN), jnp.float32),
            pltpu.VMEM((SCREENS_DEV, SCREEN, SCREEN), jnp.bfloat16),
            pltpu.VMEM((SCREENS_DEV, SCREEN, SCREEN), jnp.bfloat16),
            pltpu.VMEM((PLANES * 128, 2 * SCREEN), jnp.bfloat16),
            pltpu.VMEM((2 * SCREEN, SCREEN), jnp.bfloat16),
            pltpu.VMEM((2 * SCREEN, SCREEN), jnp.bfloat16),
            pltpu.VMEM((PLANES, SCREENS_DEV * KSIZE, 2 * SCREEN), jnp.bfloat16),
            pltpu.VMEM((SCREENS_DEV * PLANES, KSIZE, 2 * KSIZE), jnp.bfloat16),
            pltpu.SemaphoreType.DMA((16,)),
        ],
        cost_estimate=pl.CostEstimate(flops=2_700_000_000, bytes_accessed=8_600_000,
                                      transcendentals=2_000_000),
        name="screens",
    )(depths, send_list[0].T, amp, phase, jnp.asarray(dft_rows()), block_slot.reshape(3, 128),
      block_pos.reshape(3, 128), block_count)


def iota(shape, dim):
    return lax.broadcasted_iota(jnp.int32, shape, dim)


def plan_blocks(slot, pos, count):
    bins_total = 2 * POSITIONS
    slot, pos = (jnp.concatenate([v[r:r + 1] for r in range(3)], axis=1) for v in (slot, pos))
    ids = iota((1, BLOCKS_DEV), 1)
    parity = slot & 1
    used = ids < count
    bins = jnp.where(used, parity * POSITIONS + pos, -1)
    hot = (iota((bins_total, BLOCKS_DEV), 0) == bins).astype(jnp.float32)
    upto = (iota((BLOCKS_DEV, BLOCKS_DEV), 0) <= iota((BLOCKS_DEV, BLOCKS_DEV), 1)).astype(jnp.float32)
    count_to = jnp.dot(hot.astype(jnp.bfloat16), upto.astype(jnp.bfloat16),
                       preferred_element_type=jnp.float32)
    rank = jnp.sum(count_to * hot, axis=0, keepdims=True) - 1.0
    groups = jnp.floor((jnp.sum(hot, axis=1, keepdims=True) + (GROUP - 1.0)) * (1.0 / GROUP))
    wide = jnp.broadcast_to(groups, (bins_total, 128))
    b_row, b_col = iota((bins_total, bins_total), 0), iota((bins_total, bins_total), 1)
    earlier = ((b_col < b_row) & ((b_col >= POSITIONS) == (b_row >= POSITIONS))).astype(jnp.float32)
    first = jnp.dot(earlier.astype(jnp.bfloat16), wide.astype(jnp.bfloat16),
                    preferred_element_type=jnp.float32)
    last = first + wide
    place = jnp.sum(hot * first[:, :1], axis=0, keepdims=True) * GROUP + rank
    place = jnp.where(used, place.astype(jnp.int32) + parity * (MAX_GROUPS * GROUP), -1)
    high = (iota((8, BLOCKS_DEV), 0) == (place >> 7)).astype(jnp.float32)
    low = (iota((128, BLOCKS_DEV), 0) == (place & 127)).astype(jnp.float32)
    parts = [(slot >> 1).astype(jnp.float32), (ids & 127).astype(jnp.float32),
             ((ids >> 7) + 1).astype(jnp.float32)]
    spread = lax.dot_general(
        jnp.concatenate([high * part for part in parts], axis=0).astype(jnp.bfloat16),
        low.astype(jnp.bfloat16), (((1,), (1,)), ((), ())), preferred_element_type=jnp.float32)
    owner, block_low, block_high = spread[:8], spread[8:16], spread[16:]
    taken = block_high > 0.0
    owners = jnp.where(taken, owner, float(OWNERS))
    blocks = jnp.where(taken, (block_high - 1.0) * 128.0 + block_low, 0.0)
    lanes = iota((bins_total, 128), 1)
    past = (last <= lanes.astype(jnp.float32)).astype(jnp.float32)
    onto = (iota((bins_total, 128), 0) == lanes).astype(jnp.float32)
    rows = [owners, jnp.sum(past[:POSITIONS], axis=0, keepdims=True),
            jnp.sum(past[POSITIONS:], axis=0, keepdims=True),
            jnp.sum(onto * last, axis=0, keepdims=True),
            jnp.sum(onto * wide, axis=0, keepdims=True),
            jnp.sum(wide[:POSITIONS], axis=0, keepdims=True),
            jnp.sum(wide[POSITIONS:], axis=0, keepdims=True),
            jnp.zeros((2, 128), jnp.float32), blocks]
    return jnp.concatenate(rows, axis=0).astype(jnp.int32)


PLAN_ROWS = 24
ANCHORS, ENDS, GROUPS, TOTALS, BLOCKS = (row * 128 for row in (8, 10, 11, 12, 16))
LIST = MAX_GROUPS * GROUP


def lanes_low(shape):
    return lax.broadcasted_iota(jnp.int32, shape, len(shape) - 1) < KSIZE


def operator_pair(first, second):
    zero = jnp.zeros((KSIZE, 2 * KSIZE), jnp.bfloat16)
    low = lanes_low((KSIZE, 2 * KSIZE))
    turned = [jnp.concatenate([v[:, KSIZE:], v[:, :KSIZE]], axis=1) for v in (first, second)]
    left = jnp.concatenate([
        jnp.where(low, first, zero), jnp.where(low, -turned[0], zero),
        jnp.where(low, zero, turned[1]), jnp.where(low, zero, -second)], axis=0)
    right = jnp.concatenate([
        jnp.where(low, turned[0], zero), jnp.where(low, first, zero),
        jnp.where(low, zero, second), jnp.where(low, zero, turned[1])], axis=0)
    return jnp.concatenate([left, right], axis=1)


def mix_group(kernels, rows, mixed):
    for pair in range(GROUP // 2):
        two = slice(2 * pair, 2 * pair + 2)
        value = jnp.dot(jnp.concatenate(rows[two], axis=1), operator_pair(*kernels[two]),
                        preferred_element_type=jnp.float32).astype(jnp.bfloat16)
        cols = slice(pair * PATCH, (pair + 1) * PATCH)
        mixed[:PATCH, cols] = value[:, :PATCH]
        mixed[PATCH:, cols] = value[:, PATCH:]


def send_order():
    chips = [(x, y, z) for x in range(4) for y in range(4) for z in range(4)][1:]
    random.Random(0).shuffle(chips)
    order = []
    for chip in chips:
        back = tuple(-d % 4 for d in chip)
        for way in dict.fromkeys((chip, back)):
            if way + (0,) not in order:
                order += [way + (0,), way + (1,)]
    return order + [(0, 0, 0, 1)]


RING = 4
UNROLL = 4
STEPS = MAX_GROUPS // UNROLL + 1
PER_STEP = UNROLL * GROUP


def exchange_kernel(plan, even_hbm, odd_hbm, left_hbm, right_hbm, odd_out, sums_hbm,
                    recv, left, right, mixed, sums, local_sems, send_sems, recv_sems, ring_sems):
    tu, tv = lax.axis_index("tu"), lax.axis_index("tv")
    me = tu * 8 + tv
    x, z, y, core = tu // 4, tu % 4, tv // 2, tv % 2
    for source, target, c in ((even_hbm, recv, 0), (odd_hbm, odd_out, 1)):
        for dx, dy, dz, dc in send_order():
            to_u = (x + dx) % 4 * 4 + (z + dz) % 4
            to_v = (y + dy) % 4 * 2 + (core + dc) % 2
            pltpu.make_async_remote_copy(
                source.at[to_u * 8 + to_v], target.at[me], send_sems.at[c], recv_sems.at[c],
                device_id=(to_u, to_v), device_id_type=pl.DeviceIdType.MESH).start()
    own = [pltpu.make_async_copy(even_hbm.at[me], recv.at[me], local_sems.at[0]),
           pltpu.make_async_copy(odd_hbm.at[me], odd_out.at[me], local_sems.at[1]),
           pltpu.make_async_copy(left_hbm, left, local_sems.at[2]),
           pltpu.make_async_copy(right_hbm, right, local_sems.at[3])]
    for copy in own:
        copy.start()
    mixed[...] = jnp.zeros_like(mixed)
    sums[...] = jnp.zeros_like(sums)
    recv[OWNERS] = jnp.zeros_like(recv[OWNERS])
    for copy in own:
        copy.wait()
    others = pl.ds(0, OWNERS - 1)
    pltpu.make_async_copy(recv.at[others], recv.at[others], recv_sems.at[0]).wait()

    def entry(h):
        slot = lax.rem(h, RING)
        return pltpu.make_async_copy(sums.at[slot], sums_hbm.at[h], ring_sems.at[slot])

    def step(h, carry):
        @pl.when(h >= RING)
        def _():
            entry(h - RING).wait()
        slot = lax.rem(h, RING)
        before, anchors = carry
        blocks = [plan[BLOCKS + h * PER_STEP + n] for n in range(PER_STEP)]
        owners = [plan[h * PER_STEP + n] for n in range(PER_STEP)]
        patches = []
        for k in range(UNROLL):
            weights = jnp.concatenate([right[n] for n in before[k * GROUP:(k + 1) * GROUP]], axis=0)
            patches.append(jnp.dot(mixed[k], weights, preferred_element_type=jnp.float32))
        for k in range(UNROLL):
            mine = slice(k * GROUP, (k + 1) * GROUP)
            mix_group([recv[n] for n in owners[mine]], [left[n] for n in blocks[mine]], mixed.at[k])
        last = lax.rem(h + RING - 1, RING)
        same = [anchors[k] == anchors[k + 1] for k in range(UNROLL)]
        for r in range(0, 2 * PATCH, 32):
            rows = slice(r, r + 32)
            prior = sums[last, UNROLL - 1, rows]
            for k in range(UNROLL):
                prior = patches[k][rows] + jnp.where(same[k], prior, jnp.zeros_like(prior))
                sums[slot, k, rows] = prior
        entry(h).start()
        return blocks, [anchors[UNROLL]] + [plan[ANCHORS + h * UNROLL + k] for k in range(UNROLL)]
    lax.fori_loop(0, STEPS, step, ([jnp.int32(0)] * PER_STEP, [jnp.int32(0)] * (UNROLL + 1)))
    for h in range(STEPS - RING, STEPS):
        entry(h).wait()
    for c, source, target in ((0, even_hbm, recv), (1, odd_hbm, odd_out)):
        if c:
            pltpu.make_async_copy(target.at[others], target.at[others], recv_sems.at[c]).wait()
        pltpu.make_async_copy(source.at[others], source.at[others], send_sems.at[c]).wait()


def exchange(plan, even, odd, left, right):
    smem = pl.BlockSpec(memory_space=pltpu.SMEM)
    hbm = pl.BlockSpec(memory_space=pltpu.MemorySpace.HBM)
    return pl.pallas_call(
        exchange_kernel,
        out_shape=(jax.ShapeDtypeStruct(odd.shape, odd.dtype),
                   jax.ShapeDtypeStruct((STEPS, UNROLL, 2 * PATCH, PATCH), jnp.float32)),
        in_specs=[smem, hbm, hbm, hbm, hbm],
        out_specs=(hbm, hbm),
        scratch_shapes=[
            pltpu.VMEM((OWNERS + 1, *even.shape[1:]), even.dtype),
            pltpu.VMEM(left.shape, left.dtype),
            pltpu.VMEM(right.shape, right.dtype),
            pltpu.VMEM((UNROLL, 2 * PATCH, GROUP * KSIZE), jnp.bfloat16),
            pltpu.VMEM((RING, UNROLL, 2 * PATCH, PATCH), jnp.float32),
            pltpu.SemaphoreType.DMA((4,)),
            pltpu.SemaphoreType.DMA((2,)),
            pltpu.SemaphoreType.DMA((2,)),
            pltpu.SemaphoreType.DMA((RING,)),
        ],
        compiler_params=pltpu.CompilerParams(has_side_effects=True),
        name="exchange",
    )(plan, even, odd, left, right)


def turn(v):
    return pltpu.roll(v, KSIZE, 1)


def finish_kernel(plan, recv_hbm, left_hbm, right_hbm, sums_hbm, main, bottom, side,
                  recv, grid, mixed, lbuf, rbuf, sums, sems, misc_sems):
    steps = (plan[TOTALS + 128] + UNROLL - 1) // UNROLL
    received = pltpu.make_async_copy(recv_hbm, recv.at[pl.ds(0, OWNERS)], misc_sems.at[0])
    received.start()

    def start(h):
        slot = lax.rem(h, DEPTH)
        for n in range(PER_STEP):
            block = plan[BLOCKS + LIST + h * PER_STEP + n]
            pltpu.make_async_copy(left_hbm.at[block], lbuf.at[slot, n], sems.at[0, slot]).start()
            pltpu.make_async_copy(right_hbm.at[block], rbuf.at[slot, n], sems.at[1, slot]).start()

    for h in range(DEPTH - 2):
        @pl.when(h < steps)
        def _():
            start(h)

    def even_sum(q):
        at = plan[ENDS + q] - 1 + UNROLL
        return pltpu.make_async_copy(sums_hbm.at[at // UNROLL, lax.rem(at, UNROLL)], sums.at[q],
                                     misc_sems.at[1 + q])

    def start_sum(q, carry):
        @pl.when(plan[GROUPS + q] > 0)
        def _():
            even_sum(q).start()
        return carry
    lax.fori_loop(0, POSITIONS, start_sum, 0)
    grid[...] = jnp.zeros_like(grid)
    mixed[...] = jnp.zeros_like(mixed)
    rbuf[DEPTH - 1] = jnp.zeros_like(rbuf[0])
    recv[OWNERS] = jnp.zeros_like(recv[OWNERS])
    received.wait()

    def add(anchor, patch):
        row = pl.ds(pl.multiple_of((anchor >> 3) * KSIZE, KSIZE), PATCH)
        odd, col = anchor & 1, (anchor & 7) >> 1
        grid[odd, col, 0, row, :] += patch[:PATCH]
        grid[odd, col, 1, row, :] += patch[PATCH:]

    def step(h, carry):
        slot = lax.rem(h, DEPTH)

        @pl.when(h + DEPTH - 2 < steps)
        def _():
            start(h + DEPTH - 2)

        @pl.when(h < steps)
        def _():
            pltpu.make_async_copy(lbuf.at[slot], lbuf.at[slot], sems.at[0, slot]).wait()
            pltpu.make_async_copy(rbuf.at[slot], rbuf.at[slot], sems.at[1, slot]).wait()
        earlier = lax.rem(h + DEPTH - 1, DEPTH)
        patches = []
        for k in range(UNROLL):
            weights = jnp.concatenate([rbuf[earlier, k * GROUP + i] for i in range(GROUP)], axis=0)
            patches.append(jnp.dot(mixed[k], weights, preferred_element_type=jnp.float32))
        for k in range(UNROLL):
            mine = range(k * GROUP, (k + 1) * GROUP)
            mix_group([recv[plan[LIST + h * PER_STEP + n]] for n in mine],
                      [lbuf[slot, n] for n in mine], mixed.at[k])
        for k in range(UNROLL):
            add(carry[k], patches[k])
        return [jnp.minimum(plan[ANCHORS + MAX_GROUPS + h * UNROLL + k], POSITIONS - 1) for k in range(UNROLL)]

    @pl.when(steps > 0)
    def _():
        lax.fori_loop(0, steps + 1, step, [jnp.int32(0)] * UNROLL)

    def add_sum(q, carry):
        @pl.when(plan[GROUPS + q] > 0)
        def _():
            even_sum(q).wait()
            add(q, sums[q])
        return carry
    lax.fori_loop(0, POSITIONS, add_sum, 0)
    low = lanes_low((KSIZE, PATCH))
    for plane in range(2):
        for r in range(EXT_U // KSIZE):
            rows = slice(r * KSIZE, (r + 1) * KSIZE)
            shifted = [turn(grid[1, col, plane, rows, :]) for col in range(4)]
            for col in range(4):
                before = shifted[col - 1] if col else jnp.zeros_like(shifted[0])
                value = grid[0, col, plane, rows, :] + jnp.where(low, before, shifted[col])
                cols = slice(col * PATCH, (col + 1) * PATCH)
                if r < TILE_U // KSIZE:
                    main[plane, rows, cols] = value
                else:
                    bottom[plane, :, cols] = value.astype(jnp.bfloat16)
    for r in range(EXT_U // KSIZE):
        rows = slice(r * KSIZE, (r + 1) * KSIZE)
        value = jnp.where(low, turn(grid[1, 3, 0, rows, :]), grid[1, 3, 1, rows, :])
        side[rows, :] = value.astype(jnp.bfloat16)


GRID_SHAPE = (2, 4, 2, EXT_U, PATCH)


def finish(plan, recv, left, right, sums):
    vmem = pl.BlockSpec(memory_space=pltpu.VMEM)
    smem = pl.BlockSpec(memory_space=pltpu.SMEM)
    hbm = pl.BlockSpec(memory_space=pltpu.MemorySpace.HBM)
    return pl.pallas_call(
        finish_kernel,
        out_shape=(jax.ShapeDtypeStruct((2, TILE_U, TILE_V), jnp.float32),
                   jax.ShapeDtypeStruct((2, KSIZE, TILE_V), jnp.bfloat16),
                   jax.ShapeDtypeStruct((EXT_U, PATCH), jnp.bfloat16)),
        in_specs=[smem] + [hbm] * 4,
        out_specs=(vmem, vmem, vmem),
        scratch_shapes=[
            pltpu.VMEM((OWNERS + 1, *recv.shape[1:]), recv.dtype),
            pltpu.VMEM(GRID_SHAPE, jnp.float32),
            pltpu.VMEM((UNROLL, 2 * PATCH, GROUP * KSIZE), jnp.bfloat16),
            pltpu.VMEM((DEPTH, UNROLL * GROUP, PATCH, 2 * KSIZE), jnp.bfloat16),
            pltpu.VMEM((DEPTH, UNROLL * GROUP, KSIZE, PATCH), jnp.bfloat16),
            pltpu.VMEM((POSITIONS, 2 * PATCH, PATCH), jnp.float32),
            pltpu.SemaphoreType.DMA((2, DEPTH)),
            pltpu.SemaphoreType.DMA((1 + POSITIONS,)),
        ],
        cost_estimate=pl.CostEstimate(flops=1_000_000_000, bytes_accessed=12_000_000,
                                      transcendentals=0),
        name="finish",
    )(plan, recv, left, right, sums)


def border_kernel(bottom, side, bottom_out, side_out, corner_out, send_sems, recv_sems):
    tu, tv = lax.axis_index("tu"), lax.axis_index("tv")
    n_tu, n_tv = lax.axis_size("tu"), lax.axis_size("tv")
    ways = ((1, 0), (0, 1), (1, 1))
    barrier = pltpu.get_barrier_semaphore()
    for du, dv in ways:
        for sign in (1, -1):
            other = ((tu + n_tu + sign * du) % n_tu, (tv + n_tv + sign * dv) % n_tv)
            pl.semaphore_signal(barrier, inc=1, device_id=other, device_id_type=pl.DeviceIdType.MESH)
    pl.semaphore_wait(barrier, 2 * len(ways))
    parts = ((bottom, bottom_out), (side.at[pl.ds(0, TILE_U)], side_out),
             (side.at[pl.ds(TILE_U, KSIZE)], corner_out))
    copies = []
    for n, ((du, dv), (source, target)) in enumerate(zip(ways, parts)):
        copies.append(pltpu.make_async_remote_copy(
            source, target, send_sems.at[n], recv_sems.at[n],
            device_id=((tu + du) % n_tu, (tv + dv) % n_tv), device_id_type=pl.DeviceIdType.MESH))
        copies[-1].start()
    for copy in copies:
        copy.wait()


def borders(bottom, side):
    hbm = pl.BlockSpec(memory_space=pltpu.MemorySpace.HBM)
    return pl.pallas_call(
        border_kernel,
        out_shape=(jax.ShapeDtypeStruct(bottom.shape, bottom.dtype),
                   jax.ShapeDtypeStruct((TILE_U, PATCH), side.dtype),
                   jax.ShapeDtypeStruct((KSIZE, PATCH), side.dtype)),
        in_specs=[hbm, hbm],
        out_specs=(hbm,) * 3,
        scratch_shapes=[pltpu.SemaphoreType.DMA((3,)), pltpu.SemaphoreType.DMA((3,))],
        compiler_params=pltpu.CompilerParams(collective_id=1, has_side_effects=True),
        name="borders",
    )(bottom, side)


def join_kernel(main, bottom_hbm, side_hbm, corner_hbm, out, top, left, bottom, side, corner, sems):
    strips = [(top, (slice(None), pl.ds(0, KSIZE))),
              (left, (slice(None), pl.ds(KSIZE, TILE_U - KSIZE), pl.ds(0, PATCH)))]
    loads = [pltpu.make_async_copy(main.at[at], strip, sems.at[n]) for n, (strip, at) in enumerate(strips)]
    loads += [pltpu.make_async_copy(bottom_hbm, bottom, sems.at[2]),
              pltpu.make_async_copy(side_hbm, side, sems.at[3]),
              pltpu.make_async_copy(corner_hbm, corner, sems.at[4])]
    for copy in loads:
        copy.start()
    for copy in loads:
        copy.wait()
    above, beside = lax.axis_index("tu") > 0, lax.axis_index("tv") > 0

    def kept(flag, value):
        value = value.astype(jnp.float32)
        return jnp.where(flag, value, jnp.zeros_like(value))
    top[...] += kept(above, bottom[...])
    edge = kept(beside, side[...])
    tip = kept(above & beside, corner[...]) + edge[:KSIZE]
    low = lanes_low((KSIZE, PATCH))
    zero = jnp.zeros((KSIZE, PATCH), jnp.float32)
    top[0, :, :PATCH] += jnp.where(low, tip, zero)
    top[1, :, :PATCH] += jnp.where(low, turn(tip), zero)
    for r in range(1, TILE_U // KSIZE):
        rows = slice((r - 1) * KSIZE, r * KSIZE)
        part = edge[r * KSIZE:(r + 1) * KSIZE]
        left[0, rows, :] += jnp.where(low, part, zero)
        left[1, rows, :] += jnp.where(low, turn(part), zero)
    stores = [pltpu.make_async_copy(strip, out.at[at], sems.at[5 + n]) for n, (strip, at) in enumerate(strips)]
    for copy in stores:
        copy.start()
    for copy in stores:
        copy.wait()


def join(main, bottom, side, corner):
    hbm = pl.BlockSpec(memory_space=pltpu.MemorySpace.HBM)
    return pl.pallas_call(
        join_kernel,
        out_shape=jax.ShapeDtypeStruct(main.shape, main.dtype),
        in_specs=[hbm] * 4,
        out_specs=hbm,
        input_output_aliases={0: 0},
        scratch_shapes=[
            pltpu.VMEM((2, KSIZE, TILE_V), jnp.float32),
            pltpu.VMEM((2, TILE_U - KSIZE, PATCH), jnp.float32),
            pltpu.VMEM(bottom.shape, bottom.dtype),
            pltpu.VMEM(side.shape, side.dtype),
            pltpu.VMEM(corner.shape, corner.dtype),
            pltpu.SemaphoreType.DMA((7,)),
        ],
        name="join_borders",
    )(main, bottom, side, corner)


def shards(aperture_amp, aperture_phase, plane_depths, send_list, send_count, vis_left, vis_right,
           block_slot, block_pos, block_count):
    even, odd, plan = make_outgoing(plane_depths, send_list, aperture_amp, aperture_phase,
                                    block_slot, block_pos, block_count)
    plan = plan.reshape(-1)
    recv, sums = exchange(plan, even, odd, vis_left, vis_right)
    main, bottom, side = finish(plan, recv, vis_left, vis_right, sums)
    return join(main, *borders(bottom, side))


def solution(mesh):
    placed = (
        P(("tu", "tv"), None, None),
        P(("tu", "tv"), None, None),
        P(),
        P(("tu", "tv"), None, None),
        P(("tu", "tv"), None),
        P(("tu", "tv"), None, None),
        P(("tu", "tv"), None, None),
        P(("tu", "tv")),
        P(("tu", "tv")),
        P(("tu", "tv")),
    )
    return jax.shard_map(
        shards, mesh=mesh, in_specs=placed, out_specs=P(None, "tu", "tv"), check_vma=False
    )
```
